128 devices in a mesh: ctx: 8 (over z, core), head: 16 (over x, y).
Axes of the slice: x: 4, y: 4, z: 4, core: 2. Of those that a mesh axis runs over, the one named last changes fastest.
Arguments:
- queries: bfloat16 [24576, 8192], P('ctx', 'head'), may hold values from -64 to 64
- key_vectors: bfloat16 [24576, 8192], P('ctx', 'head'), may hold values from -5 to 5
- value_vectors: bfloat16 [24576, 8192], P('ctx', 'head'), may hold values from -6 to 6
- step_sizes: float32 [16, 24576], P('head', 'ctx'), may hold values from 0.0003 to 0.003
- w_in: bfloat16 [16, 512, 512], P('head'), may hold values from -0.25 to 0.25
- w_up: bfloat16 [16, 512, 512], P('head'), may hold values from -0.25 to 0.25
- w_out: bfloat16 [16, 512, 512], P('head'), may hold values from -0.125 to 0.125
- out_gate: bfloat16 [24576, 8192], P('ctx', 'head'), may hold values from -6 to 6
- norm_gain: float32 [8192], replicated, may hold values from 0.5 to 1.5
Outputs:
- layer_out: bfloat16 [24576, 8192], P(('ctx', 'head'))
The draws below stay inside these ranges and needn't reach their ends.
All inputs are finite; a program needn't handle non-finite values.
Results may differ from the reference program's by a relative error of at most 0.025.
Values may be sent and summed in bfloat16 or wider, within the bound.
No kernel may reach another device: no remote copies, remote signals or barrier semaphores. Data moves between devices by JAX's collectives and lax.ppermute only.
A program may use at most 128 MiB of HBM per device.

```python
import math
import jax
import jax.numpy as jnp
from jax import lax

HD = 512
FH = 512
WINDOW = 1024
TOK_DEV = 3072
HEADS = 16
D = 8192
TOKENS = 24576
N_CTX = 8


def drawn_field(key, salt, limit):
    return jnp.clip(jax.random.normal(jax.random.fold_in(key, salt), (TOKENS, D), jnp.float32), -limit, limit)


def draw_queries(key, part):
    return drawn_field(key, 12, 4.0).astype(jnp.bfloat16)


def draw_key_vectors(key, part):
    return drawn_field(key, 11, 4.0).astype(jnp.bfloat16)


def shard_levels(key, extent, cuts, least, high):
    def one(axis_at, parts):
        steps = jax.random.uniform(jax.random.fold_in(jax.random.fold_in(key, 6), axis_at), (parts,), jnp.float32, least / len(cuts), high / len(cuts))
        return jnp.repeat(jnp.exp(steps), extent[axis_at] // parts).reshape((-1,) + (1,) * (len(extent) - axis_at - 1))

    loudness = one(*cuts[0])
    for cut in cuts[1:]:
        loudness = loudness * one(*cut)
    return loudness


def noise(own_key, extent, spread, most, shards=(), held_as=jnp.bfloat16):
    factor_of = shard_levels(own_key, extent, shards, -0.22, 0.18) if shards else 1.0
    entries = jax.random.normal(own_key, extent, jnp.float32) * spread * factor_of
    return jnp.minimum(jnp.maximum(entries, -most), most).astype(held_as)


def setup_inputs(seed: int = 0) -> dict:
    arg_keys = jax.random.split(jax.random.key(seed), 10)
    queries = draw_queries(jax.random.fold_in(arg_keys[9], 71), 0)
    key_vectors = draw_key_vectors(jax.random.fold_in(arg_keys[9], 71), 0)
    value_vectors = noise(arg_keys[2], (TOKENS, D), 1.0, 6.0, ((0, 8), (1, 16)))
    step_sizes = jnp.clip(jnp.exp(math.log(0.003) - 2.3025851 * jax.random.uniform(arg_keys[3], (HEADS, TOKENS), jnp.float32) ** shard_levels(arg_keys[3], (HEADS, TOKENS), ((0, 16), (1, 8)), -0.2, 0.2)), 0.0003, 0.003)
    w_in = noise(arg_keys[4], (HEADS, HD, FH), HD ** -0.5, 0.25, ((0, 16),))
    w_up = noise(arg_keys[5], (HEADS, HD, FH), HD ** -0.5, 0.25, ((0, 16),))
    w_out = noise(arg_keys[6], (HEADS, HD, FH), (4 * FH) ** -0.5, 0.125, ((0, 16),))
    out_gate = noise(arg_keys[7], (TOKENS, D), 1.0, 6.0, ((0, 8), (1, 16)))
    norm_gain = jnp.clip(1.0 + 0.1 * jax.random.normal(arg_keys[8], (D,), jnp.float32), 0.5, 1.5)
    return {"queries": queries, "key_vectors": key_vectors, "value_vectors": value_vectors, "step_sizes": step_sizes, "w_in": w_in, "w_up": w_up, "w_out": w_out, "out_gate": out_gate, "norm_gain": norm_gain}


EPSILON = 1e-06

def silu_slope(pre):
    sigmoid = jax.nn.sigmoid(pre)
    return sigmoid * (1.0 + pre * (1.0 - sigmoid))

def block_attention(query_rows, key_rows, value_rows, first_query, first_key):
    scores = jnp.dot(query_rows, key_rows.T, preferred_element_type=jnp.float32) * query_rows.shape[1] ** (-0.5)
    query_pos = first_query + jnp.arange(query_rows.shape[0], dtype=jnp.int32)[:, None]
    key_pos = first_key + jnp.arange(key_rows.shape[0], dtype=jnp.int32)[None, :]
    distance = query_pos - key_pos
    allowed = (distance >= 0) & (distance < WINDOW) & (key_pos >= 0)
    masked = jnp.where(allowed, scores, -1e+30)
    largest = lax.optimization_barrier(jnp.max(masked, axis=1, keepdims=True))
    powered = jnp.where(allowed, jnp.exp(masked - largest), 0.0)
    weights = (powered / lax.optimization_barrier(jnp.sum(powered, axis=1, keepdims=True))).astype(jnp.bfloat16)
    return jnp.dot(weights, value_rows, preferred_element_type=jnp.float32)

def fast_increments(key_rows, value_rows, rate_rows, w_in, w_up, w_out):
    pre_gate = jnp.dot(key_rows, w_in, preferred_element_type=jnp.float32)
    pre_up = jnp.dot(key_rows, w_up, preferred_element_type=jnp.float32)
    hidden = (jax.nn.silu(pre_gate) * pre_up).astype(jnp.bfloat16)
    scaled = (rate_rows[:, None] * value_rows.astype(jnp.float32)).astype(jnp.bfloat16)
    backward = jnp.dot(scaled, w_out, preferred_element_type=jnp.float32)
    grad_gate = (backward * pre_up * silu_slope(pre_gate)).astype(jnp.bfloat16)
    grad_up = (backward * jax.nn.silu(pre_gate)).astype(jnp.bfloat16)
    return (jnp.dot(key_rows.T, grad_gate, preferred_element_type=jnp.float32), jnp.dot(key_rows.T, grad_up, preferred_element_type=jnp.float32), jnp.dot(scaled.T, hidden, preferred_element_type=jnp.float32))

def renormed(initial, increment):
    initial_f = initial.astype(jnp.float32)
    updated = initial_f + increment
    rescale = jnp.sqrt(lax.optimization_barrier(jnp.mean(initial_f * initial_f, axis=0)) + EPSILON) / jnp.sqrt(lax.optimization_barrier(jnp.mean(updated * updated, axis=0)) + EPSILON)
    return (updated * rescale).astype(jnp.bfloat16)

def apply_fast(query_rows, new_in, new_up, new_out):
    hidden = (jax.nn.silu(jnp.dot(query_rows, new_in, preferred_element_type=jnp.float32)) * jnp.dot(query_rows, new_up, preferred_element_type=jnp.float32)).astype(jnp.bfloat16)
    return lax.dot_general(hidden, new_out, (((1,), (1,)), ((), ())), preferred_element_type=jnp.float32)

def gated_norm(combined, out_gate, norm_gain):
    values_f = combined.astype(jnp.float32)
    mean_sq = lax.optimization_barrier(jnp.mean(values_f * values_f, axis=1, keepdims=True))
    return (values_f * lax.rsqrt(mean_sq + EPSILON) * norm_gain.astype(jnp.float32) * jax.nn.silu(out_gate.astype(jnp.float32))).astype(jnp.bfloat16)

def reference(queries, key_vectors, value_vectors, step_sizes, w_in, w_up, w_out, out_gate, norm_gain):
    head_count = w_in.shape[0]
    head_width = w_in.shape[1]

    def per_head(head_index):
        column_start = head_index * head_width
        q_head = lax.dynamic_slice_in_dim(queries, column_start, head_width, 1)
        k_head = lax.dynamic_slice_in_dim(key_vectors, column_start, head_width, 1)
        v_head = lax.dynamic_slice_in_dim(value_vectors, column_start, head_width, 1)
        rate_head = step_sizes[head_index]
        padded_keys = jnp.concatenate([jnp.zeros((WINDOW, head_width), k_head.dtype), k_head], axis=0)
        padded_values = jnp.concatenate([jnp.zeros((WINDOW, head_width), v_head.dtype), v_head], axis=0)

        def one_block(block_index):
            first = block_index * WINDOW
            q_rows = lax.dynamic_slice_in_dim(q_head, first, WINDOW, 0)
            k_rows = lax.dynamic_slice_in_dim(padded_keys, first, 2 * WINDOW, 0)
            v_rows = lax.dynamic_slice_in_dim(padded_values, first, 2 * WINDOW, 0)
            return block_attention(q_rows, k_rows, v_rows, first, first - WINDOW)
        attended = lax.map(one_block, jnp.arange(TOKENS // WINDOW, dtype=jnp.int32)).reshape(TOKENS, head_width)

        def one_shard(shard_index):
            first = shard_index * TOK_DEV
            partial_value = fast_increments(lax.dynamic_slice_in_dim(k_head, first, TOK_DEV, 0), lax.dynamic_slice_in_dim(v_head, first, TOK_DEV, 0), lax.dynamic_slice_in_dim(rate_head, first, TOK_DEV, 0), w_in[head_index], w_up[head_index], w_out[head_index])
            return (partial_value[0].astype(jnp.bfloat16), partial_value[1].astype(jnp.bfloat16), partial_value[2].astype(jnp.bfloat16))
        pieces = lax.map(one_shard, jnp.arange(N_CTX, dtype=jnp.int32))
        new_in = renormed(w_in[head_index], lax.optimization_barrier(jnp.sum(pieces[0].astype(jnp.float32), axis=0)))
        new_up = renormed(w_up[head_index], lax.optimization_barrier(jnp.sum(pieces[1].astype(jnp.float32), axis=0)))
        new_out = renormed(w_out[head_index], lax.optimization_barrier(jnp.sum(pieces[2].astype(jnp.float32), axis=0)))
        return (attended + apply_fast(q_head, new_in, new_up, new_out)).astype(jnp.bfloat16)
    heads_out = lax.map(per_head, jnp.arange(head_count, dtype=jnp.int32))
    combined = jnp.transpose(heads_out, (1, 0, 2)).reshape(TOKENS, head_count * head_width)
    return gated_norm(combined, out_gate, norm_gain)
```

```python
import functools

import jax
import jax.numpy as jnp
from jax import lax
from jax.experimental import pallas as pl
from jax.experimental.pallas import tpu as pltpu
from jax.sharding import PartitionSpec as P


WINDOW = 1024
EPSILON = 1e-06
LOG2E = 1.4426950408889634


F32 = jnp.float32
BF16 = jnp.bfloat16
NT = (((1,), (1,)), ((), ()))


def sigmoid(x):
    return 0.5 * jnp.tanh(0.5 * x) + 0.5


def dot_nt(a, b):
    return lax.dot_general(a, b, NT, preferred_element_type=F32)


def dot_nn(a, b):
    return jnp.dot(a, b, preferred_element_type=F32)


def whole(shape):
    return pl.BlockSpec(shape, lambda *_: (0,) * len(shape))


def increments_kernel(pos, k_ref, v_ref, rate_ref, wi_ref, wu_ref, wo_ref,
                      keep_ref, send_ref, slice_ref, wt, acc):
    step = pl.program_id(0)
    tile = k_ref.shape[0]

    @pl.when(step == 0)
    def _():
        wt[0] = wi_ref[0].T
        wt[1] = wu_ref[0].T
        wt[2] = wo_ref[0].T
        acc[...] = jnp.zeros_like(acc)

    k = k_ref[...]
    rate = jnp.broadcast_to(rate_ref[...], (128, tile)).T
    rate = jnp.concatenate([rate] * (v_ref.shape[1] // 128), axis=1)
    scaled = (rate * v_ref[...].astype(F32)).astype(BF16)
    gate = dot_nt(wt[0], k)
    up = dot_nt(wt[1], k)
    back = dot_nt(wt[2], scaled)
    sig = sigmoid(gate)
    act = gate * sig
    hidden = (act * up).astype(BF16)
    grad_gate = (back * up * (sig * (1.0 + gate * (1.0 - sig)))).astype(BF16)
    grad_up = (back * act).astype(BF16)
    acc[0] += dot_nn(grad_gate, k)
    acc[1] += dot_nn(grad_up, k)
    acc[2] += dot_nn(hidden, scaled)

    @pl.when(step == pl.num_programs(0) - 1)
    def _():
        half = keep_ref.shape[1]
        part = slice_ref.shape[1]
        mine = pl.multiple_of(pos[1] * half, half)
        other = pl.multiple_of((1 - pos[1]) * half, half)
        keep_ref[...] = acc[:, pl.ds(mine, half), :].astype(BF16)
        send_ref[...] = acc[:, pl.ds(other, half), :].astype(BF16)
        own = pl.multiple_of(pos[1] * half + pos[0] * part, part)
        slice_ref[...] = wt[:, pl.ds(own, part), :]


def increments(pos, k, v, rate, w_in, w_up, w_out, z_size):
    rows, hd = k.shape
    fh = w_in.shape[2]
    tile = 512
    half, part = fh // 2, fh // 2 // z_size
    row_spec = pl.BlockSpec((tile, hd), lambda i, *_: (i, 0))
    w_spec = whole((1, hd, fh))
    return pl.pallas_call(
        increments_kernel,
        grid_spec=pltpu.PrefetchScalarGridSpec(
            num_scalar_prefetch=1,
            grid=(rows // tile,),
            in_specs=[row_spec, row_spec, pl.BlockSpec((1, tile), lambda i, *_: (0, i)),
                      w_spec, w_spec, w_spec],
            out_specs=[whole((3, half, hd)), whole((3, half, hd)), whole((3, part, hd))],
            scratch_shapes=[pltpu.VMEM((3, fh, hd), BF16), pltpu.VMEM((3, fh, hd), F32)],
        ),
        out_shape=[jax.ShapeDtypeStruct((3, half, hd), BF16),
                   jax.ShapeDtypeStruct((3, half, hd), BF16),
                   jax.ShapeDtypeStruct((3, part, hd), BF16)],
        cost_estimate=pl.CostEstimate(flops=12 * rows * hd * fh, bytes_accessed=9 << 20,
                                      transcendentals=rows * fh),
        name="increments",
    )(pos, k, v, rate, w_in, w_up, w_out)


def pair_sum_kernel(pos, keep_ref, got_ref, *outs):
    count = len(outs)
    part = outs[0].shape[1]
    for d in range(count):
        at = pl.multiple_of(lax.rem(pos[0] + d, count) * part, part)
        rows = pl.ds(at, part)
        outs[d][...] = (keep_ref[:, rows, :].astype(F32) + got_ref[:, rows, :].astype(F32)).astype(BF16)


def pair_sum(pos, keep, got, z_size):
    three, half, hd = keep.shape
    part = half // z_size
    return pl.pallas_call(
        pair_sum_kernel,
        grid_spec=pltpu.PrefetchScalarGridSpec(
            num_scalar_prefetch=1, grid=(1,),
            in_specs=[whole(keep.shape)] * 2,
            out_specs=[whole((three, part, hd))] * z_size,
        ),
        out_shape=[jax.ShapeDtypeStruct((three, part, hd), BF16)] * z_size,
        name="pair_sum",
    )(pos, keep, got)


def renorm_kernel(w_ref, *refs):
    parts, out_ref = refs[:-1], refs[-1]
    w = w_ref[...].astype(F32)
    total = parts[0][...].astype(F32)
    for p in parts[1:]:
        total = total + p[...].astype(F32)
    updated = w + total
    size = w.shape[-1]
    before = jnp.sum(w * w, axis=-1, keepdims=True) / size + EPSILON
    after = jnp.sum(updated * updated, axis=-1, keepdims=True) / size + EPSILON
    out_ref[...] = (updated * (jnp.sqrt(before) / jnp.sqrt(after))).astype(BF16)


def renormed(w, parts):
    return pl.pallas_call(
        renorm_kernel,
        out_shape=jax.ShapeDtypeStruct(w.shape, BF16),
        name="renorm",
    )(w, *parts)


def attend_rows(q, k_at, v_at, lo, first, scale):
    tq = q.shape[0]
    blocks = WINDOW // tq + 1
    row = lax.broadcasted_iota(jnp.int32, (tq, tq), 0)
    col = lax.broadcasted_iota(jnp.int32, (tq, tq), 1)
    scores = []
    for j in range(blocks):
        s = dot_nt(q, k_at(j))
        ok = None
        if j == 0:
            ok = col > row
        if j == blocks - 1:
            ok = col <= row
        if lo is not None and j < blocks - 1:
            inside = col >= lo - (first + j * tq)
            ok = inside if ok is None else ok & inside
        scores.append(s if ok is None else jnp.where(ok, s, -1e30))
    top = functools.reduce(jnp.maximum, scores)
    top = jnp.max(top, axis=1, keepdims=True) * scale
    out, total = None, None
    for j in range(blocks):
        p = jnp.exp2(scores[j] * scale - top)
        total = p if total is None else total + p
        o = dot_nn(p.astype(BF16), v_at(j))
        out = o if out is None else out + o
    return out / jnp.sum(total, axis=1, keepdims=True)


def attention_own_kernel(q_ref, k_ref, v_ref, o_ref, *, tq, skip, scale):
    step = pl.program_id(0)
    per = q_ref.shape[0] // tq
    for n in range(per):
        base = (step + skip) * per * tq + n * tq - WINDOW

        def at(ref, j):
            return ref[pl.ds(pl.multiple_of(base + j * tq, tq), tq), :]

        o_ref[n * tq:(n + 1) * tq, :] = attend_rows(
            q_ref[n * tq:(n + 1) * tq, :], lambda j: at(k_ref, j), lambda j: at(v_ref, j),
            None, None, scale).astype(BF16)


def attention_first_kernel(pos, q_ref, kb_ref, vb_ref, k_ref, v_ref, _, o_ref, ek, ev, *, tq, scale):
    step = pl.program_id(0)

    @pl.when(step == 0)
    def _():
        ek[:WINDOW, :] = kb_ref[...]
        ek[WINDOW:, :] = k_ref[...]
        ev[:WINDOW, :] = vb_ref[...]
        ev[WINDOW:, :] = v_ref[...]

    lo = jnp.where(pos[0] + pos[1] == 0, WINDOW, 0)
    per = q_ref.shape[0] // tq
    for n in range(per):
        base = step * per * tq + n * tq

        def at(ref, j):
            return ref[pl.ds(pl.multiple_of(base + j * tq, tq), tq), :]

        o_ref[n * tq:(n + 1) * tq, :] = attend_rows(
            q_ref[n * tq:(n + 1) * tq, :], lambda j: at(ek, j), lambda j: at(ev, j),
            lo, base, scale).astype(BF16)


def attention_own(q, k, v, tq=256, tile=512):
    rows, hd = q.shape
    skip = WINDOW // tile
    scale = hd ** -0.5 * LOG2E
    count = rows // tile - skip
    tile_spec = pl.BlockSpec((tile, hd), lambda i: (i + skip, 0))
    return pl.pallas_call(
        functools.partial(attention_own_kernel, tq=tq, skip=skip, scale=scale),
        grid=(count,),
        in_specs=[tile_spec, whole((rows, hd)), whole((rows, hd))],
        out_specs=tile_spec,
        out_shape=jax.ShapeDtypeStruct((rows, hd), BF16),
        cost_estimate=pl.CostEstimate(flops=4 * count * tile * (WINDOW + tq) * hd,
                                      bytes_accessed=10 << 20, transcendentals=count * tile * WINDOW),
        name="attention_own",
    )(q, k, v)


def attention_first(pos, q, k_before, v_before, k, v, attended, tq=256, tile=512):
    hd = q.shape[1]
    scale = hd ** -0.5 * LOG2E
    count = WINDOW // tile
    tile_spec = pl.BlockSpec((tile, hd), lambda i, *_: (i, 0))
    return pl.pallas_call(
        functools.partial(attention_first_kernel, tq=tq, scale=scale),
        grid_spec=pltpu.PrefetchScalarGridSpec(
            num_scalar_prefetch=1, grid=(count,),
            in_specs=[tile_spec] + [whole((WINDOW, hd))] * 4 + [pl.BlockSpec(memory_space=pl.ANY)],
            out_specs=tile_spec,
            scratch_shapes=[pltpu.VMEM((2 * WINDOW, hd), BF16)] * 2,
        ),
        out_shape=jax.ShapeDtypeStruct(attended.shape, BF16),
        input_output_aliases={6: 0},
        cost_estimate=pl.CostEstimate(flops=4 * WINDOW * (WINDOW + tq) * hd,
                                      bytes_accessed=6 << 20, transcendentals=WINDOW * WINDOW),
        name="attention_first",
    )(pos, q, k_before, v_before, k, v, attended)


EXTRA = 8
LANES = 256


def apply_kernel(pos, q_ref, attended_ref, gate_ref, gain_ref, *refs):
    pieces, (y_ref, wt) = refs[:-2], refs[-2:]
    step = pl.program_id(0)

    @pl.when(step == 0)
    def _():
        at = 0
        for p in pieces:
            rows = p.shape[1]
            wt[:, at:at + rows, :] = p[...]
            at += rows

    q = q_ref[...]
    gate = dot_nt(q, wt[0])
    up = dot_nt(q, wt[1])
    hidden = (gate * sigmoid(gate) * up).astype(BF16)
    fast = dot_nn(hidden, wt[2])
    head = (attended_ref[...].astype(F32) + fast).astype(BF16).astype(F32)
    squares = jnp.sum(head * head, axis=1, keepdims=True)
    g = gate_ref[...].astype(F32)
    y = (head * (gain_ref[...] * (g * sigmoid(g)))).astype(BF16)
    share = y_ref.shape[1] - EXTRA
    for n in range(y_ref.shape[0]):
        rows = slice(n * share, (n + 1) * share)
        y_ref[n, :share, :] = y[rows]
        column = jnp.concatenate([squares[rows], jnp.zeros((LANES - share, 1), F32)], axis=0)
        line = jnp.broadcast_to(column, (LANES, 128)).T[:EXTRA, :]
        high = line.astype(BF16)
        low = (line - high.astype(F32)).astype(BF16)
        y_ref[n, share:, :LANES] = high
        y_ref[n, share:, LANES:] = low


def applied(pos, q, attended, out_gate, gain, pieces, n_head, per=4):
    rows, hd = q.shape
    share = rows // n_head
    tile = per * share
    fh = sum(p.shape[1] for p in pieces)
    row_spec = pl.BlockSpec((tile, hd), lambda i, *_: (i, 0))
    return pl.pallas_call(
        apply_kernel,
        grid_spec=pltpu.PrefetchScalarGridSpec(
            num_scalar_prefetch=1, grid=(n_head // per,),
            in_specs=[row_spec, row_spec, row_spec,
                      pl.BlockSpec((1, hd), lambda i, pos: (0, pos[2]))] + [whole(p.shape) for p in pieces],
            out_specs=pl.BlockSpec((per, share + EXTRA, hd), lambda i, *_: (i, 0, 0)),
            scratch_shapes=[pltpu.VMEM((3, fh, hd), BF16)],
        ),
        out_shape=jax.ShapeDtypeStruct((n_head, share + EXTRA, hd), BF16),
        cost_estimate=pl.CostEstimate(flops=6 * rows * hd * fh, bytes_accessed=14 << 20,
                                      transcendentals=2 * rows * fh),
        name="apply_fast",
    )(pos, q, attended, out_gate, gain, *pieces)


def scale_kernel(y_ref, squares_ref, o_ref, factor):
    share = o_ref.shape[0]

    @pl.when(pl.program_id(0) == 0)
    def _():
        s = squares_ref[...].astype(F32)
        line = jnp.sum(s, axis=0)
        line = line[:, :LANES] + line[:, LANES:]
        r = lax.rsqrt(line / (s.shape[0] * s.shape[2]) + EPSILON)
        factor[...] = jnp.concatenate([r] * (128 // EXTRA), axis=0).T

    r = factor[:share, :]
    width = y_ref.shape[2]
    r = jnp.concatenate([r] * (width // 128), axis=1)
    for h in range(y_ref.shape[0]):
        o_ref[:, h * width:(h + 1) * width] = (y_ref[h, :share, :].astype(F32) * r).astype(BF16)


def scaled_rows(y, per=4):
    heads, rows, hd = y.shape
    share = rows - EXTRA
    return pl.pallas_call(
        scale_kernel,
        grid=(heads // per,),
        in_specs=[pl.BlockSpec((per, rows, hd), lambda i: (i, 0, 0)),
                  pl.BlockSpec((heads, EXTRA, hd), lambda i: (0, share // EXTRA, 0))],
        out_specs=pl.BlockSpec((share, per * hd), lambda i: (0, i)),
        out_shape=jax.ShapeDtypeStruct((share, heads * hd), BF16),
        scratch_shapes=[pltpu.VMEM((LANES, 128), F32)],
        name="scale_rows",
    )(y, y)


def layer(queries, key_vectors, value_vectors, step_sizes, w_in, w_up, w_out, out_gate, norm_gain):
    rows, _ = queries.shape
    n_ctx, n_head = lax.axis_size("ctx"), lax.axis_size("head")
    z_size = n_ctx // 2
    ctx = lax.axis_index("ctx")
    pos = jnp.stack([ctx >> 1, ctx & 1, lax.axis_index("head")]).astype(jnp.int32)
    tied = lax.optimization_barrier

    onward = [(i, i + 1) for i in range(n_ctx - 1)]
    k_before = lax.ppermute(key_vectors[rows - WINDOW:], "ctx", onward)
    v_before = lax.ppermute(value_vectors[rows - WINDOW:], "ctx", onward)

    keep, send, w_slice = increments(pos, key_vectors, value_vectors, step_sizes, w_in, w_up, w_out, z_size)
    partner = [(i, i ^ 1) for i in range(n_ctx)]

    def along_z(d):
        return [(i, ((i // 2 + d) % z_size) * 2 + i % 2) for i in range(n_ctx)]

    got = lax.ppermute(send, "ctx", partner)
    parts = pair_sum(pos, keep, got, z_size)
    order = sorted(range(1, z_size), key=lambda d: -min(d, z_size - d))
    arrived = [lax.ppermute(parts[d], "ctx", along_z(d)) for d in order]
    q_own, own_part = tied((queries, parts[0]))
    attended = attention_own(q_own, key_vectors, value_vectors)
    attended, arrived = tied((attended, arrived))
    new_piece = renormed(w_slice, [own_part] + arrived)
    rest = [lax.ppermute(new_piece, "ctx", along_z(d)) for d in order]
    q_first, own_piece = tied((queries, new_piece))
    attended = attention_first(pos, q_first, k_before, v_before, key_vectors, value_vectors, attended)
    attended, rest = tied((attended, rest))
    chip = [own_piece] + rest
    other = [lax.ppermute(p, "ctx", partner) for p in chip]

    y = applied(pos, queries, attended, out_gate, norm_gain.reshape(1, -1), chip + other, n_head)
    y = lax.all_to_all(y, "head", split_axis=0, concat_axis=0, tiled=True)
    return scaled_rows(y)


def solution(mesh):
    return jax.shard_map(
        layer,
        mesh=mesh,
        in_specs=(
            P("ctx", "head"), P("ctx", "head"), P("ctx", "head"), P("head", "ctx"),
            P("head", None, None), P("head", None, None), P("head", None, None),
            P("ctx", "head"), P(),
        ),
        out_specs=P(("ctx", "head"), None),
        check_vma=False,
    )
```

```python
import functools

import jax
import jax.numpy as jnp
from jax import lax
from jax.experimental import pallas as pl
from jax.experimental.pallas import tpu as pltpu
from jax.sharding import PartitionSpec as P


WINDOW = 1024
EPSILON = 1e-06
LOG2E = 1.4426950408889634


F32 = jnp.float32
BF16 = jnp.bfloat16
NT = (((1,), (1,)), ((), ()))


def sigmoid(x):
    return 0.5 * jnp.tanh(0.5 * x) + 0.5


def silu(x):
    half = 0.5 * x
    return half * jnp.tanh(half) + half


def dot_nt(a, b):
    return lax.dot_general(a, b, NT, preferred_element_type=F32)


def dot_nn(a, b):
    return jnp.dot(a, b, preferred_element_type=F32)


def whole(shape):
    return pl.BlockSpec(shape, lambda *_: (0,) * len(shape))


def increments_kernel(table, k_ref, v_ref, rate_ref, wi_ref, wu_ref, wo_ref,
                      keep_ref, send_ref, slice_ref, wt, acc):
    step = pl.program_id(0)
    tile = k_ref.shape[0]

    @pl.when(step == 0)
    def _():
        wt[0] = wi_ref[0].T
        wt[1] = wu_ref[0].T
        wt[2] = wo_ref[0].T

    k = k_ref[...]
    rate = jnp.broadcast_to(rate_ref[...], (128, tile)).T
    rate = jnp.concatenate([rate] * (v_ref.shape[1] // 128), axis=1)
    scaled = (rate * v_ref[...].astype(F32)).astype(BF16)
    gate = dot_nt(wt[0], k)
    up = dot_nt(wt[1], k)
    back = dot_nt(wt[2], scaled)
    sig = sigmoid(gate)
    act = gate * sig
    hidden = (act * up).astype(BF16)
    grad_gate = (back * up * (sig + act * (1.0 - sig))).astype(BF16)
    grad_up = (back * act).astype(BF16)
    first = step == 0
    acc[0] = jnp.where(first, 0.0, acc[0]) + dot_nn(grad_gate, k)
    acc[1] = jnp.where(first, 0.0, acc[1]) + dot_nn(grad_up, k)
    acc[2] = jnp.where(first, 0.0, acc[2]) + dot_nn(hidden, scaled)

    @pl.when(step == pl.num_programs(0) - 1)
    def _():
        half = keep_ref.shape[1]
        part = slice_ref.shape[1]
        mine = pl.multiple_of(table[CORE_AT] * half, half)
        other = pl.multiple_of((1 - table[CORE_AT]) * half, half)
        keep_ref[...] = acc[:, pl.ds(mine, half), :].astype(BF16)
        send_ref[...] = acc[:, pl.ds(other, half), :].astype(BF16)
        own = pl.multiple_of(table[CORE_AT] * half + table[Z_AT] * part, part)
        slice_ref[...] = wt[:, pl.ds(own, part), :]


def increments(table, k, v, rate, w_in, w_up, w_out, z_size):
    rows, hd = k.shape
    fh = w_in.shape[2]
    tile = 512
    half, part = fh // 2, fh // 2 // z_size
    row_spec = pl.BlockSpec((tile, hd), lambda i, *_: (i, 0))
    w_spec = whole((1, hd, fh))
    return pl.pallas_call(
        increments_kernel,
        grid_spec=pltpu.PrefetchScalarGridSpec(
            num_scalar_prefetch=1,
            grid=(rows // tile,),
            in_specs=[row_spec, row_spec, pl.BlockSpec((1, tile), lambda i, *_: (0, i)),
                      w_spec, w_spec, w_spec],
            out_specs=[whole((3, half, hd)), whole((3, half, hd)), whole((3, part, hd))],
            scratch_shapes=[pltpu.VMEM((3, fh, hd), BF16), pltpu.VMEM((3, fh, hd), F32)],
        ),
        out_shape=[jax.ShapeDtypeStruct((3, half, hd), BF16),
                   jax.ShapeDtypeStruct((3, half, hd), BF16),
                   jax.ShapeDtypeStruct((3, part, hd), BF16)],
        cost_estimate=pl.CostEstimate(flops=12 * rows * hd * fh, bytes_accessed=9 << 20,
                                      transcendentals=rows * fh),
        compiler_params=pltpu.CompilerParams(vmem_limit_bytes=28 << 20),
        name="increments",
    )(table, k, v, rate, w_in, w_up, w_out)


def pair_sum_kernel(table, keep_ref, got_ref, *outs):
    count = len(outs)
    part = outs[0].shape[1]
    for d in range(count):
        at = pl.multiple_of(lax.rem(table[Z_AT] + d, count) * part, part)
        rows = pl.ds(at, part)
        outs[d][...] = (keep_ref[:, rows, :].astype(F32) + got_ref[:, rows, :].astype(F32)).astype(BF16)


def pair_sum(table, keep, got, z_size):
    three, half, hd = keep.shape
    part = half // z_size
    return pl.pallas_call(
        pair_sum_kernel,
        grid_spec=pltpu.PrefetchScalarGridSpec(
            num_scalar_prefetch=1, grid=(1,),
            in_specs=[whole(keep.shape)] * 2,
            out_specs=[whole((three, part, hd))] * z_size,
        ),
        out_shape=[jax.ShapeDtypeStruct((three, part, hd), BF16)] * z_size,
        compiler_params=pltpu.CompilerParams(vmem_limit_bytes=8 << 20),
        name="pair_sum",
    )(table, keep, got)


def renorm_kernel(w_ref, *refs):
    parts, out_ref = refs[:-1], refs[-1]
    w = w_ref[...].astype(F32)
    total = parts[0][...].astype(F32)
    for p in parts[1:]:
        total = total + p[...].astype(F32)
    updated = w + total
    size = w.shape[-1]
    before = jnp.sum(w * w, axis=-1, keepdims=True) / size + EPSILON
    after = jnp.sum(updated * updated, axis=-1, keepdims=True) / size + EPSILON
    out_ref[...] = (updated * (jnp.sqrt(before) / jnp.sqrt(after))).astype(BF16)


def renormed(w, parts):
    return pl.pallas_call(
        renorm_kernel,
        out_shape=jax.ShapeDtypeStruct(w.shape, BF16),
        compiler_params=pltpu.CompilerParams(vmem_limit_bytes=8 << 20),
        name="renorm",
    )(w, *parts)


SIDE = 4
SHIFTS = ((1, 1), (3, 3), (2, 2), (1, 3), (3, 1), (2, 1), (1, 2), (3, 2),
          (2, 3), (2, 0), (0, 2), (1, 0), (0, 1), (3, 0), (0, 3), (0, 0))
GROUPS = (2, 4, 4, 6)
Z_AT, CORE_AT, HEAD_AT, TARGET_AT = 0, 1, 2, 3
SOURCE_AT = TARGET_AT + len(SHIFTS)


def shifted(h, dx, dy):
    return (h // SIDE + dx) % SIDE * SIDE + (h + dy) % SIDE


def load_kernel(*refs, count):
    ins, outs, (tail_ref, table, sems) = refs[:count], refs[count:2 * count], refs[2 * count:]
    rows = ins[0].shape[0]
    late, early = pl.ds(rows - WINDOW, WINDOW), pl.ds(0, rows - WINDOW)

    def moved(src, dst, n):
        c = pltpu.make_async_copy(src, dst, sems.at[n])
        c.start()
        return c

    firsts = [moved(ins[n].at[late], outs[n].at[late], n) for n in range(2)]
    rest = [moved(ins[n].at[early], outs[n].at[early], 2 + n) for n in range(2)]
    rest += [moved(ins[n], outs[n], 2 + n) for n in range(2, count)]
    ctx, head = lax.axis_index("ctx"), lax.axis_index("head")
    table[Z_AT], table[CORE_AT], table[HEAD_AT] = ctx // 2, ctx % 2, head
    for n, (dx, dy) in enumerate(SHIFTS):
        table[TARGET_AT + n] = shifted(head, dx, dy)
        table[SOURCE_AT + n] = shifted(head, SIDE - dx, SIDE - dy)
    for n, c in enumerate(firsts):
        c.wait()
        rest.append(moved(outs[n].at[late], tail_ref.at[n], 2 + count + n))
    for c in rest:
        c.wait()


def loaded(*arrays):
    _, hd = arrays[0].shape
    count = len(arrays)
    anywhere = pl.BlockSpec(memory_space=pl.ANY)
    return pl.pallas_call(
        functools.partial(load_kernel, count=count),
        in_specs=[anywhere] * count,
        out_specs=[pl.BlockSpec(memory_space=pltpu.VMEM)] * count
        + [anywhere, pl.BlockSpec(memory_space=pltpu.SMEM)],
        out_shape=[pltpu.VMEM(a.shape, a.dtype) for a in arrays]
        + [jax.ShapeDtypeStruct((2, WINDOW, hd), BF16), jax.ShapeDtypeStruct((SOURCE_AT + len(SHIFTS),), jnp.int32)],
        scratch_shapes=[pltpu.SemaphoreType.DMA((4 + count,))],
        compiler_params=pltpu.CompilerParams(vmem_limit_bytes=54 << 20),
        name="load_rows",
    )(*arrays)


def attend_rows(q, k, v, lo, scale):
    tq, span = q.shape[0], k.shape[0]
    row = lax.broadcasted_iota(jnp.int32, (tq, tq), 0)
    col = lax.broadcasted_iota(jnp.int32, (tq, tq), 1)
    s = dot_nt(q, k)
    if lo is not None:
        s = jnp.where(lax.broadcasted_iota(jnp.int32, (tq, span), 1) >= lo, s, -1e30)
    parts = [jnp.where(col > row, s[:, :tq], -1e30), s[:, tq:WINDOW], jnp.where(col <= row, s[:, WINDOW:], -1e30)]
    top = jnp.maximum(jnp.max(jnp.maximum(parts[0], parts[2]), axis=1, keepdims=True),
                      jnp.max(parts[1], axis=1, keepdims=True)) * scale
    p = jnp.concatenate([jnp.exp2(x * scale - top) for x in parts], axis=1)
    total = jnp.sum(p, axis=1, keepdims=True)
    return dot_nn(p.astype(BF16), v) * (1.0 / total)


def attention_own_kernel(q_ref, k_ref, v_ref, *refs, tq, skip, scale):
    o_ref = refs[-1]
    per = q_ref.shape[0] // tq
    for n in range(per):
        base = pl.multiple_of((pl.program_id(0) + skip) * per * tq + n * tq - WINDOW, tq)
        rows = slice(n * tq, (n + 1) * tq)
        keys = pl.ds(base, WINDOW + tq)
        o_ref[rows, :] = attend_rows(q_ref[rows, :], k_ref[keys, :], v_ref[keys, :], None, scale).astype(BF16)


def attention_first_kernel(table, q_ref, b_ref, k_ref, v_ref, _, o_ref, ek, ev, sems, *, tq, scale):
    step = pl.program_id(0)

    @pl.when(step == 0)
    def _():
        copies = [
            pltpu.make_async_copy(b_ref.at[0], ek.at[pl.ds(0, WINDOW)], sems.at[0]),
            pltpu.make_async_copy(k_ref.at[pl.ds(0, WINDOW)], ek.at[pl.ds(WINDOW, WINDOW)], sems.at[1]),
            pltpu.make_async_copy(b_ref.at[1], ev.at[pl.ds(0, WINDOW)], sems.at[2]),
            pltpu.make_async_copy(v_ref.at[pl.ds(0, WINDOW)], ev.at[pl.ds(WINDOW, WINDOW)], sems.at[3]),
        ]
        for c in copies:
            c.start()
        for c in copies:
            c.wait()

    limit = jnp.where(table[Z_AT] + table[CORE_AT] == 0, WINDOW, 0)
    per = q_ref.shape[0] // tq
    for n in range(per):
        base = pl.multiple_of(step * per * tq + n * tq, tq)
        rows = slice(n * tq, (n + 1) * tq)
        keys = pl.ds(base, WINDOW + tq)
        o_ref[rows, :] = attend_rows(q_ref[rows, :], ek[keys, :], ev[keys, :], limit - base, scale).astype(BF16)


def attention_own(q, k, v, start, stop, attended=None, tq=256, tile=512):
    rows, hd = q.shape
    skip = start // tile
    scale = hd ** -0.5 * LOG2E
    count = (stop - start) // tile
    tile_spec = pl.BlockSpec((tile, hd), lambda i: (i + skip, 0))
    into = [] if attended is None else [attended]
    return pl.pallas_call(
        functools.partial(attention_own_kernel, tq=tq, skip=skip, scale=scale),
        grid=(count,),
        in_specs=[tile_spec, whole((rows, hd)), whole((rows, hd))] + [pl.BlockSpec(memory_space=pl.ANY)] * len(into),
        out_specs=tile_spec,
        out_shape=jax.ShapeDtypeStruct((rows, hd), BF16),
        input_output_aliases={3: 0} if into else {},
        cost_estimate=pl.CostEstimate(flops=4 * count * tile * (WINDOW + tq) * hd,
                                      bytes_accessed=10 << 20, transcendentals=count * tile * WINDOW),
        compiler_params=pltpu.CompilerParams(vmem_limit_bytes=24 << 20),
        name="attention_own",
    )(q, k, v, *into)


def attention_first(table, q, before, k, v, attended, tq=256, tile=512):
    hd = q.shape[1]
    scale = hd ** -0.5 * LOG2E
    count = WINDOW // tile
    tile_spec = pl.BlockSpec((tile, hd), lambda i, *_: (i, 0))
    return pl.pallas_call(
        functools.partial(attention_first_kernel, tq=tq, scale=scale),
        grid_spec=pltpu.PrefetchScalarGridSpec(
            num_scalar_prefetch=1, grid=(count,),
            in_specs=[tile_spec] + [pl.BlockSpec(memory_space=pl.ANY)] * 4,
            out_specs=tile_spec,
            scratch_shapes=[pltpu.VMEM((2 * WINDOW, hd), BF16)] * 2 + [pltpu.SemaphoreType.DMA((4,))],
        ),
        out_shape=jax.ShapeDtypeStruct(attended.shape, BF16),
        input_output_aliases={5: 0},
        cost_estimate=pl.CostEstimate(flops=4 * WINDOW * (WINDOW + tq) * hd,
                                      bytes_accessed=6 << 20, transcendentals=WINDOW * WINDOW),
        compiler_params=pltpu.CompilerParams(vmem_limit_bytes=20 << 20),
        name="attention_first",
    )(table, q, before, k, v, attended)


EXTRA = 8
LANES = 256


def apply_kernel(*refs, count, n_pieces):
    refs = refs[1:]
    q_refs, attended_refs, gate_refs = refs[:count], refs[count:2 * count], refs[2 * count:3 * count]
    gain_ref, weights, outs = refs[3 * count], refs[3 * count + 1:3 * count + 1 + n_pieces], refs[3 * count + 1 + n_pieces:]
    if n_pieces > 1:
        wt, start = outs[-1], 0
        for p in weights:
            wt[:, start:start + p.shape[1], :] = p[...]
            start += p.shape[1]
    else:
        wt = weights[0]
    share = q_refs[0].shape[1]
    q = jnp.concatenate([r[0] for r in q_refs], axis=0)
    hidden = (silu(dot_nt(q, wt[0])) * dot_nt(q, wt[1])).astype(BF16)
    fast = dot_nn(hidden, wt[2])
    for n in range(count):
        rows = slice(n * share, (n + 1) * share)
        head = (attended_refs[n][0].astype(F32) + fast[rows]).astype(BF16).astype(F32)
        squares = jnp.sum(head * head, axis=1, keepdims=True)
        y = outs[n]
        y[:share, :] = (head * (gain_ref[...] * silu(gate_refs[n][0].astype(F32)))).astype(BF16)
        column = jnp.concatenate([squares, jnp.zeros((LANES - share, 1), F32)], axis=0)
        line = jnp.broadcast_to(column, (LANES, 128)).T[:EXTRA, :]
        high = line.astype(BF16)
        low = (line - high.astype(F32)).astype(BF16)
        y[share:, :LANES] = high
        y[share:, LANES:] = low


def applied(table, q, attended, out_gate, gain, weights, n_head, at, count):
    rows, hd = q.shape
    share = rows // n_head
    fh = sum(p.shape[1] for p in weights)
    blocks = [a.reshape(n_head, share, hd) for a in (q, attended, out_gate)]
    specs = [pl.BlockSpec((1, share, hd), lambda i, t, j=TARGET_AT + at + j: (t[j], 0, 0)) for j in range(count)]
    first = len(weights) > 1
    outs = [jax.ShapeDtypeStruct((share + EXTRA, hd), BF16)] * count
    outs += [jax.ShapeDtypeStruct((3, fh, hd), BF16)] * first
    return pl.pallas_call(
        functools.partial(apply_kernel, count=count, n_pieces=len(weights)),
        grid_spec=pltpu.PrefetchScalarGridSpec(
            num_scalar_prefetch=1, grid=(1,),
            in_specs=specs * 3 + [pl.BlockSpec((1, hd), lambda i, t: (0, t[HEAD_AT]))] + [whole(p.shape) for p in weights],
            out_specs=[whole(o.shape) for o in outs],
        ),
        out_shape=outs,
        cost_estimate=pl.CostEstimate(flops=6 * count * share * hd * fh, bytes_accessed=count << 20,
                                      transcendentals=2 * count * share * fh),
        compiler_params=pltpu.CompilerParams(vmem_limit_bytes=18 << 20),
        name="apply_fast",
    )(table, *[b for b in blocks for _ in range(count)], gain, *weights)


def scale_kernel(table, *refs):
    count = (len(refs) - 2) // 1 - 1
    y_refs, (o_ref, buf, sems) = refs[:count], refs[count:]
    share, width = buf.shape[1:]
    s = y_refs[0][share:, :].astype(F32)
    for y in y_refs[1:]:
        s = s + y[share:, :].astype(F32)
    line = s[:, :LANES] + s[:, LANES:]
    r = lax.rsqrt(line / (count * width) + EPSILON)
    r = jnp.concatenate([r] * (128 // EXTRA), axis=0).T[:share, :]
    r = jnp.concatenate([r] * (width // 128), axis=1)
    copies = []
    for n in range(count):
        buf[n] = (y_refs[n][:share, :].astype(F32) * r).astype(BF16)
        columns = pl.ds(pl.multiple_of(table[SOURCE_AT + n] * width, width), width)
        copies.append(pltpu.make_async_copy(buf.at[n], o_ref.at[:, columns], sems.at[n]))
        copies[-1].start()
    for c in copies:
        c.wait()


def scaled_rows(table, parts):
    rows, hd = parts[0].shape
    share, count = rows - EXTRA, len(parts)
    return pl.pallas_call(
        scale_kernel,
        grid_spec=pltpu.PrefetchScalarGridSpec(
            num_scalar_prefetch=1, grid=(1,),
            in_specs=[whole((rows, hd))] * count,
            out_specs=pl.BlockSpec(memory_space=pl.ANY),
            scratch_shapes=[pltpu.VMEM((count, share, hd), BF16), pltpu.SemaphoreType.DMA((count,))],
        ),
        out_shape=jax.ShapeDtypeStruct((share, count * hd), BF16),
        compiler_params=pltpu.CompilerParams(vmem_limit_bytes=16 << 20),
        name="scale_rows",
    )(table, *parts)


def layer(queries, key_vectors, value_vectors, step_sizes, w_in, w_up, w_out, out_gate, norm_gain):
    rows, _ = queries.shape
    n_ctx, n_head = lax.axis_size("ctx"), lax.axis_size("head")
    z_size = n_ctx // 2
    tied = lax.optimization_barrier

    key_vectors, value_vectors, w_in, w_up, w_out, tail, table = loaded(key_vectors, value_vectors, w_in, w_up, w_out)
    before = lax.ppermute(tail, "ctx", [(i, i + 1) for i in range(n_ctx - 1)])
    keep, send, w_slice = increments(table, key_vectors, value_vectors, step_sizes, w_in, w_up, w_out, z_size)
    partner = [(i, i ^ 1) for i in range(n_ctx)]

    def along_z(d):
        return [(i, ((i // 2 + d) % z_size) * 2 + i % 2) for i in range(n_ctx)]

    got = lax.ppermute(send, "ctx", partner)
    parts = pair_sum(table, keep, got, z_size)
    order = sorted(range(1, z_size), key=lambda d: -min(d, z_size - d))
    arrived = [lax.ppermute(parts[d], "ctx", along_z(d)) for d in order]
    q_own, own_part = tied((queries, parts[0]))
    cut = rows - WINDOW // 2
    attended = attention_own(q_own, key_vectors, value_vectors, WINDOW, cut)
    attended, arrived = tied((attended, arrived))
    new_piece = renormed(w_slice, [own_part] + arrived)
    rest = [lax.ppermute(new_piece, "ctx", along_z(d)) for d in order]
    q_first, own_piece = tied((queries, new_piece))
    attended = attention_own(q_first, key_vectors, value_vectors, cut, rows, attended)
    attended = attention_first(table, q_first, before, key_vectors, value_vectors, attended)
    attended, rest = tied((attended, rest))
    chip = [own_piece] + rest
    other = [lax.ppermute(p, "ctx", partner) for p in chip]

    weights, gain = chip + other, norm_gain.reshape(1, -1)
    parts, at = [], 0
    for count in GROUPS:
        outs = applied(table, queries, attended, out_gate, gain, weights, n_head, at, count)
        if len(outs) > count:
            weights = outs[count:]
        for y, (dx, dy) in zip(outs, SHIFTS[at:at + count]):
            if dx or dy:
                y = lax.ppermute(y, "head", [(h, shifted(h, dx, dy)) for h in range(n_head)])
            parts.append(y)
        at += count
    return scaled_rows(table, parts)


def solution(mesh):
    return jax.shard_map(
        layer,
        mesh=mesh,
        in_specs=(
            P("ctx", "head"), P("ctx", "head"), P("ctx", "head"), P("head", "ctx"),
            P("head", None, None), P("head", None, None), P("head", None, None),
            P("ctx", "head"), P(),
        ),
        out_specs=P(("ctx", "head"), None),
        check_vma=False,
    )
```

```python
import functools

import jax
import jax.numpy as jnp
from jax import lax
from jax.experimental import pallas as pl
from jax.experimental.pallas import tpu as pltpu
from jax.sharding import PartitionSpec as P


WINDOW = 1024
EPSILON = 1e-06
LOG2E = 1.4426950408889634


F32 = jnp.float32
BF16 = jnp.bfloat16
NT = (((1,), (1,)), ((), ()))


def sigmoid(x):
    return 0.5 * jnp.tanh(0.5 * x) + 0.5


def silu(x):
    half = 0.5 * x
    return half * jnp.tanh(half) + half


def dot_nt(a, b):
    return lax.dot_general(a, b, NT, preferred_element_type=F32)


def dot_nn(a, b):
    return jnp.dot(a, b, preferred_element_type=F32)


def whole(shape):
    return pl.BlockSpec(shape, lambda *_: (0,) * len(shape))


def position():
    ctx = lax.axis_index("ctx")
    return ctx // 2, ctx % 2


TILE = 512


STEP = 1024


def increments_kernel(k_hbm, v_hbm, rate_ref, wi_hbm, wu_hbm, wo_hbm,
                      keep_ref, send_ref, slice_ref, k_ref, v_ref, w, wt, acc, w_sems, sems):
    rows = k_ref.shape[0]
    loads = [pltpu.make_async_copy(src.at[0], w.at[n], w_sems.at[n]) for n, src in enumerate((wi_hbm, wu_hbm, wo_hbm))]

    def tile_loads(t):
        at = pl.ds(pl.multiple_of(t * TILE, TILE), TILE)
        return (pltpu.make_async_copy(k_hbm.at[at], k_ref.at[at], sems.at[2 * t]),
                pltpu.make_async_copy(v_hbm.at[at], v_ref.at[at], sems.at[2 * t + 1]))

    ahead = 2
    for c in loads:
        c.start()
    for t in range(ahead):
        for c in tile_loads(t):
            c.start()
    for n, c in enumerate(loads):
        c.wait()
        wt[n] = w[n].T
    for t in range(ahead, rows // TILE):
        for c in tile_loads(t):
            c.start()

    def one(t, carry):
        for n in range(STEP // TILE):
            for c in tile_loads(t * (STEP // TILE) + n):
                c.wait()
        at = pl.ds(pl.multiple_of(t * STEP, STEP), STEP)
        k = k_ref[at, :]
        rate = jnp.broadcast_to(rate_ref[:, at], (128, STEP)).T
        rate = jnp.concatenate([rate] * (v_ref.shape[1] // 128), axis=1)
        scaled = (rate * v_ref[at, :].astype(F32)).astype(BF16)
        gate = dot_nt(wt[0], k)
        up = dot_nt(wt[1], k)
        back = dot_nt(wt[2], scaled)
        sig = sigmoid(gate)
        act = gate * sig
        hidden = (act * up).astype(BF16)
        grad_gate = (back * up * (sig + act * (1.0 - sig))).astype(BF16)
        grad_up = (back * act).astype(BF16)
        first = t == 0
        acc[0] = jnp.where(first, 0.0, acc[0]) + dot_nn(grad_gate, k)
        acc[1] = jnp.where(first, 0.0, acc[1]) + dot_nn(grad_up, k)
        acc[2] = jnp.where(first, 0.0, acc[2]) + dot_nn(hidden, scaled)
        return carry

    lax.fori_loop(0, rows // STEP, one, 0)
    z, core = position()
    half, part = keep_ref.shape[1], slice_ref.shape[1]
    mine = pl.multiple_of(core * half, half)
    other = pl.multiple_of((1 - core) * half, half)
    send_ref[...] = acc[:, pl.ds(other, half), :].astype(BF16)
    keep_ref[...] = acc[:, pl.ds(mine, half), :].astype(BF16)
    slice_ref[...] = wt[:, pl.ds(pl.multiple_of(core * half + z * part, part), part), :]


def increments(k, v, rate, w_in, w_up, w_out, z_size):
    rows, hd = k.shape
    fh = w_in.shape[2]
    half, part = fh // 2, fh // 2 // z_size
    anywhere, inside = pl.BlockSpec(memory_space=pl.ANY), pl.BlockSpec(memory_space=pltpu.VMEM)
    return pl.pallas_call(
        increments_kernel,
        in_specs=[anywhere, anywhere, inside, anywhere, anywhere, anywhere],
        out_specs=[inside] * 5,
        out_shape=[pltpu.VMEM((3, half, hd), BF16), pltpu.VMEM((3, half, hd), BF16), pltpu.VMEM((3, part, hd), BF16),
                   pltpu.VMEM((rows, hd), BF16), pltpu.VMEM((rows, hd), BF16)],
        scratch_shapes=[pltpu.VMEM((3, hd, fh), BF16), pltpu.VMEM((3, fh, hd), BF16), pltpu.VMEM((3, fh, hd), F32),
                        pltpu.SemaphoreType.DMA((3,)), pltpu.SemaphoreType.DMA((2 * rows // TILE,))],
        cost_estimate=pl.CostEstimate(flops=12 * rows * hd * fh, bytes_accessed=9 << 20,
                                      transcendentals=rows * fh),
        compiler_params=pltpu.CompilerParams(vmem_limit_bytes=48 << 20),
        name="increments",
    )(k, v, rate, w_in, w_up, w_out)


def small_call(kernel, outs, *args):
    return pl.pallas_call(kernel, out_shape=outs, compiler_params=pltpu.CompilerParams(vmem_limit_bytes=8 << 20))(*args)


def pair_sum_kernel(keep_ref, got_ref, *outs):
    count = len(outs)
    part = outs[0].shape[1]
    z, _ = position()
    for d in range(count):
        rows = pl.ds(pl.multiple_of((z + d) % count * part, part), part)
        outs[d][...] = (keep_ref[:, rows, :].astype(F32) + got_ref[:, rows, :].astype(F32)).astype(BF16)


def pair_sum(keep, got, z_size):
    three, half, hd = keep.shape
    return small_call(pair_sum_kernel, [jax.ShapeDtypeStruct((three, half // z_size, hd), BF16)] * z_size,
                      keep, got)


def renorm_kernel(w_ref, *refs):
    parts, out_ref = refs[:-1], refs[-1]
    w = w_ref[...].astype(F32)
    total = parts[0][...].astype(F32)
    for p in parts[1:]:
        total = total + p[...].astype(F32)
    updated = w + total
    size = w.shape[-1]
    before = jnp.sum(w * w, axis=-1, keepdims=True) / size + EPSILON
    after = jnp.sum(updated * updated, axis=-1, keepdims=True) / size + EPSILON
    out_ref[...] = (updated * (jnp.sqrt(before) / jnp.sqrt(after))).astype(BF16)


SIDE = 4
SHIFTS = ((1, 1), (3, 3), (2, 2), (1, 3), (3, 1), (2, 1), (1, 2), (3, 2),
          (2, 3), (2, 0), (0, 2), (1, 0), (0, 1), (3, 0), (0, 3), (0, 0))
GROUPS = (2, 4, 4, 5, 1)
HEAD_AT, TARGET_AT = 0, 1
SOURCE_AT = TARGET_AT + len(SHIFTS)


def shifted(h, dx, dy):
    return (h // SIDE + dx) % SIDE * SIDE + (h + dy) % SIDE


def tail_kernel(k_ref, v_ref, tail_ref, table, sems):
    rows = pl.ds(k_ref.shape[0] - WINDOW, WINDOW)
    copies = [pltpu.make_async_copy(ref.at[rows], tail_ref.at[n], sems.at[n]) for n, ref in enumerate((k_ref, v_ref))]
    for c in copies:
        c.start()
    head = lax.axis_index("head")
    table[HEAD_AT] = head
    for n, (dx, dy) in enumerate(SHIFTS):
        table[TARGET_AT + n] = shifted(head, dx, dy)
        table[SOURCE_AT + n] = shifted(head, SIDE - dx, SIDE - dy)
    for c in copies:
        c.wait()


def tails(k, v):
    hd = k.shape[1]
    return pl.pallas_call(
        tail_kernel,
        in_specs=[pl.BlockSpec(memory_space=pl.ANY)] * 2,
        out_specs=[pl.BlockSpec(memory_space=pltpu.VMEM), pl.BlockSpec(memory_space=pltpu.SMEM)],
        out_shape=[pltpu.VMEM((2, WINDOW, hd), BF16), jax.ShapeDtypeStruct((SOURCE_AT + len(SHIFTS),), jnp.int32)],
        scratch_shapes=[pltpu.SemaphoreType.DMA((2,))],
        compiler_params=pltpu.CompilerParams(vmem_limit_bytes=60 << 20),
        name="tails",
    )(k, v)


def softmax_parts(s, lo, scale):
    tq, span = s.shape[0], s.shape[1]
    row = lax.broadcasted_iota(jnp.int32, (tq, tq), 0)
    col = lax.broadcasted_iota(jnp.int32, (tq, tq), 1)
    if lo is not None:
        s = jnp.where(lax.broadcasted_iota(jnp.int32, (tq, span), 1) >= lo, s, -1e30)
    parts = [jnp.where(col > row, s[:, :tq], -1e30), s[:, tq:WINDOW], jnp.where(col <= row, s[:, WINDOW:], -1e30)]
    top = jnp.maximum(jnp.max(jnp.maximum(parts[0], parts[2]), axis=1, keepdims=True),
                      jnp.max(parts[1], axis=1, keepdims=True)) * scale
    p = jnp.concatenate([jnp.exp2(x * scale - top) for x in parts], axis=1)
    return p.astype(BF16), 1.0 / jnp.sum(p, axis=1, keepdims=True)


def attend(q_ref, o_ref, key_rows, value_rows, lo, tq, scale):
    count = q_ref.shape[0] // tq

    def rows(n):
        return slice(n * tq, (n + 1) * tq)

    scores = dot_nt(q_ref[rows(0), :], key_rows(0))
    for n in range(count):
        ahead = dot_nt(q_ref[rows(n + 1), :], key_rows(n + 1)) if n + 1 < count else None
        p, inverse = softmax_parts(scores, None if lo is None else lo - n * tq, scale)
        o_ref[rows(n), :] = (dot_nn(p, value_rows(n)) * inverse).astype(BF16)
        scores = ahead


def attention_own_kernel(q_ref, k_ref, v_ref, *refs, tq, skip, scale):
    def window(ref):
        def rows(n):
            base = (pl.program_id(0) + skip) * q_ref.shape[0] + n * tq - WINDOW
            return ref[pl.ds(pl.multiple_of(base, tq), WINDOW + tq), :]

        return rows

    attend(q_ref, refs[-1], window(k_ref), window(v_ref), None, tq, scale)


def attention_first_kernel(q_ref, b_ref, k_ref, v_ref, *refs, at, tq, scale):
    o_ref, ek, ev, sems = refs[-4:]
    old, new = WINDOW - at, ek.shape[0] - WINDOW + at
    copies = []
    for n, (keys, held) in enumerate(((k_ref, ek), (v_ref, ev))):
        copies.append(pltpu.make_async_copy(b_ref.at[n, pl.ds(at, old)], held.at[pl.ds(0, old)], sems.at[2 * n]))
        copies.append(pltpu.make_async_copy(keys.at[pl.ds(0, new)], held.at[pl.ds(old, new)], sems.at[2 * n + 1]))
    for c in copies:
        c.start()
    for c in copies:
        c.wait()
    z, core = position()
    lo = jnp.where(z + core == 0, WINDOW, 0) - at

    def window(ref):
        return lambda n: ref[n * tq:n * tq + WINDOW + tq, :]

    attend(q_ref, o_ref, window(ek), window(ev), lo, tq, scale)


def attention_own(q, k, v, start, stop, attended=None, tq=256, tile=512):
    rows, hd = q.shape
    skip = start // tile
    scale = hd ** -0.5 * LOG2E
    count = (stop - start) // tile
    tile_spec = pl.BlockSpec((tile, hd), lambda i: (i + skip, 0))
    into = [] if attended is None else [attended]
    return pl.pallas_call(
        functools.partial(attention_own_kernel, tq=tq, skip=skip, scale=scale),
        grid=(count,),
        in_specs=[tile_spec, whole((rows, hd)), whole((rows, hd))] + [pl.BlockSpec(memory_space=pl.ANY)] * len(into),
        out_specs=tile_spec,
        out_shape=jax.ShapeDtypeStruct((rows, hd), BF16),
        input_output_aliases={3: 0} if into else {},
        cost_estimate=pl.CostEstimate(flops=4 * count * tile * (WINDOW + tq) * hd,
                                      bytes_accessed=10 << 20, transcendentals=count * tile * WINDOW),
        compiler_params=pltpu.CompilerParams(vmem_limit_bytes=24 << 20),
        name="attention_own",
    )(q, k, v, *into)


def attention_first(q, before, k, v, attended, at, tq=256, tile=512):
    hd = q.shape[1]
    scale = hd ** -0.5 * LOG2E
    tile_spec = pl.BlockSpec((tile, hd), lambda i: (at // tile, 0))
    return pl.pallas_call(
        functools.partial(attention_first_kernel, at=at, tq=tq, scale=scale),
        grid=(1,),
        in_specs=[tile_spec] + [pl.BlockSpec(memory_space=pl.ANY)] * 4,
        out_specs=tile_spec,
        scratch_shapes=[pltpu.VMEM((WINDOW + tile, hd), BF16)] * 2 + [pltpu.SemaphoreType.DMA((4,))],
        out_shape=jax.ShapeDtypeStruct(attended.shape, BF16),
        input_output_aliases={4: 0},
        cost_estimate=pl.CostEstimate(flops=4 * tile * (WINDOW + tq) * hd,
                                      bytes_accessed=4 << 20, transcendentals=tile * WINDOW),
        compiler_params=pltpu.CompilerParams(vmem_limit_bytes=20 << 20),
        name="attention_first",
    )(q, before, k, v, attended)


EXTRA = 8
LANES = 256


def apply_kernel(*refs, count, n_pieces, at):
    refs = refs[1:]
    q_refs, attended_refs, gate_refs = refs[:count], refs[count:2 * count], refs[2 * count:3 * count]
    gain_ref, weights, outs = refs[3 * count], refs[3 * count + 1:3 * count + 1 + n_pieces], refs[3 * count + 1 + n_pieces:]
    if n_pieces > 1:
        wt, start = outs[-1], 0
        for p in weights:
            wt[:, start:start + p.shape[1], :] = p[...]
            start += p.shape[1]
    else:
        wt = weights[0]
    share = q_refs[0].shape[1]
    q = jnp.concatenate([r[0] for r in q_refs], axis=0)
    hidden = (silu(dot_nt(q, wt[0])) * dot_nt(q, wt[1])).astype(BF16)
    fast = dot_nn(hidden, wt[2])
    for n in range(count):
        rows = slice(n * share, (n + 1) * share)
        head = (attended_refs[n][0].astype(F32) + fast[rows]).astype(BF16).astype(F32)
        squares = jnp.sum(head * head, axis=1, keepdims=True)
        y = outs[n]
        y[:share, :] = (head * (gain_ref[...] * silu(gate_refs[n][0].astype(F32)))).astype(BF16)
        column = jnp.concatenate([squares, jnp.zeros((LANES - share, 1), F32)], axis=0)
        line = jnp.broadcast_to(column, (LANES, 128)).T[:EXTRA, :]
        high = line.astype(BF16)
        low = (line - high.astype(F32)).astype(BF16)
        y[share:, :LANES] = high
        y[share:, LANES:] = low


def applied(table, q, attended, out_gate, gain, weights, n_head, at, count):
    rows, hd = q.shape
    share = rows // n_head
    fh = sum(p.shape[1] for p in weights)
    blocks = [a.reshape(n_head, share, hd) for a in (q, attended, out_gate)]
    specs = [pl.BlockSpec((1, share, hd), lambda i, t, j=TARGET_AT + at + j: (t[j], 0, 0)) for j in range(count)]
    first = len(weights) > 1
    outs = [jax.ShapeDtypeStruct((share + EXTRA, hd), BF16)] * count
    outs += [jax.ShapeDtypeStruct((3, fh, hd), BF16)] * first
    return pl.pallas_call(
        functools.partial(apply_kernel, count=count, n_pieces=len(weights), at=at),
        grid_spec=pltpu.PrefetchScalarGridSpec(
            num_scalar_prefetch=1, grid=(1,),
            in_specs=specs * 3 + [pl.BlockSpec((1, hd), lambda i, t: (0, t[HEAD_AT]))] + [whole(p.shape) for p in weights],
            out_specs=[whole(o.shape) for o in outs],
        ),
        out_shape=outs,
        cost_estimate=pl.CostEstimate(flops=6 * count * share * hd * fh, bytes_accessed=count << 20,
                                      transcendentals=2 * count * share * fh),
        compiler_params=pltpu.CompilerParams(vmem_limit_bytes=18 << 20),
        name="apply_fast",
    )(table, *[b for b in blocks for _ in range(count)], gain, *weights)


def scale_kernel(table, *refs):
    count = (len(refs) - 2) // 1 - 1
    y_refs, (o_ref, buf, sems) = refs[:count], refs[count:]
    share, width = buf.shape[1:]
    s = y_refs[0][share:, :].astype(F32)
    for y in y_refs[1:]:
        s = s + y[share:, :].astype(F32)
    line = s[:, :LANES] + s[:, LANES:]
    r = lax.rsqrt(line / (count * width) + EPSILON)
    r = jnp.concatenate([r] * (128 // EXTRA), axis=0).T[:share, :]
    r = jnp.concatenate([r] * (width // 128), axis=1)
    copies = []
    for n in range(count):
        buf[n] = (y_refs[n][:share, :].astype(F32) * r).astype(BF16)
        columns = pl.ds(pl.multiple_of(table[SOURCE_AT + n] * width, width), width)
        copies.append(pltpu.make_async_copy(buf.at[n], o_ref.at[:, columns], sems.at[n]))
        copies[-1].start()
    for c in copies:
        c.wait()


def scaled_rows(table, parts):
    rows, hd = parts[0].shape
    share, count = rows - EXTRA, len(parts)
    return pl.pallas_call(
        scale_kernel,
        grid_spec=pltpu.PrefetchScalarGridSpec(
            num_scalar_prefetch=1, grid=(1,),
            in_specs=[whole((rows, hd))] * count,
            out_specs=pl.BlockSpec(memory_space=pl.ANY),
            scratch_shapes=[pltpu.VMEM((count, share, hd), BF16), pltpu.SemaphoreType.DMA((count,))],
        ),
        out_shape=jax.ShapeDtypeStruct((share, count * hd), BF16),
        compiler_params=pltpu.CompilerParams(vmem_limit_bytes=16 << 20),
        name="scale_rows",
    )(table, *parts)


def layer(queries, key_vectors, value_vectors, step_sizes, w_in, w_up, w_out, out_gate, norm_gain):
    rows, _ = queries.shape
    n_ctx, n_head = lax.axis_size("ctx"), lax.axis_size("head")
    z_size = n_ctx // 2
    tied = lax.optimization_barrier

    def along_z(x, d):
        return lax.ppermute(x, "ctx", [(i, ((i // 2 + d) % z_size) * 2 + i % 2) for i in range(n_ctx)])

    def swapped(x):
        return lax.ppermute(x, "ctx", [(i, i ^ 1) for i in range(n_ctx)])

    tail, table = tails(key_vectors, value_vectors)
    before = lax.ppermute(tail, "ctx", [(i, i + 1) for i in range(n_ctx - 1)])
    keep, send, w_slice, keys, values = increments(
        key_vectors, value_vectors, step_sizes, w_in, w_up, w_out, z_size)

    order = sorted(range(1, z_size), key=lambda d: -min(d, z_size - d))
    parts = pair_sum(keep, swapped(send), z_size)
    arrived = [along_z(parts[d], d) for d in order]
    q, own = tied((queries, parts[0]))
    attended = attention_own(q, keys, values, WINDOW, rows)
    attended, arrived = tied((attended, arrived))
    piece = small_call(renorm_kernel, jax.ShapeDtypeStruct(own.shape, BF16), w_slice, own, *arrived)
    rest = [along_z(piece, d) for d in order]
    q, piece = tied((queries, piece))
    attended = attention_first(q, before, keys, values, attended, 0)
    attended = attention_first(q, before, keys, values, attended, TILE)
    attended, rest = tied((attended, rest))
    chip = [piece] + rest
    other = [swapped(p) for p in chip]

    weights, gain = chip + other, norm_gain.reshape(1, -1)
    parts, at = [], 0
    for count in GROUPS:
        outs = applied(table, queries, attended, out_gate, gain, weights, n_head, at, count)
        if len(outs) > count:
            weights = outs[count:]
        for y, (dx, dy) in zip(outs, SHIFTS[at:at + count]):
            if dx or dy:
                y = lax.ppermute(y, "head", [(h, shifted(h, dx, dy)) for h in range(n_head)])
            parts.append(y)
        at += count
    return scaled_rows(table, parts)


def solution(mesh):
    return jax.shard_map(
        layer,
        mesh=mesh,
        in_specs=(
            P("ctx", "head"), P("ctx", "head"), P("ctx", "head"), P("head", "ctx"),
            P("head", None, None), P("head", None, None), P("head", None, None),
            P("ctx", "head"), P(),
        ),
        out_specs=P(("ctx", "head"), None),
        check_vma=False,
    )
```

```python
import functools

import jax
import jax.numpy as jnp
from jax import lax
from jax.experimental import pallas as pl
from jax.experimental.pallas import tpu as pltpu
from jax.sharding import PartitionSpec as P


WINDOW = 1024
EPSILON = 1e-06
LOG2E = 1.4426950408889634


F32 = jnp.float32
BF16 = jnp.bfloat16
NT = (((1,), (1,)), ((), ()))


def sigmoid(x):
    return 0.5 * jnp.tanh(0.5 * x) + 0.5


def silu(x):
    half = 0.5 * x
    return half * jnp.tanh(half) + half


def dot_nt(a, b):
    return lax.dot_general(a, b, NT, preferred_element_type=F32)


def dot_nn(a, b):
    return jnp.dot(a, b, preferred_element_type=F32)


def position():
    ctx = lax.axis_index("ctx")
    return ctx // 2, ctx % 2


TILE = 512


STEP = 1024


def increments_kernel(k_hbm, v_hbm, rate_ref, wi_ref, wu_ref, wo_ref,
                      keep_ref, send_ref, slice_ref, k_ref, v_ref, wt, acc, sems):
    rows = k_ref.shape[0]

    def tile_loads(t):
        at = pl.ds(pl.multiple_of(t * TILE, TILE), TILE)
        return (pltpu.make_async_copy(k_hbm.at[at], k_ref.at[at], sems.at[2 * t]),
                pltpu.make_async_copy(v_hbm.at[at], v_ref.at[at], sems.at[2 * t + 1]))

    ahead = STEP // TILE
    for t in range(ahead):
        for c in tile_loads(t):
            c.start()
    for n, w in enumerate((wi_ref, wu_ref, wo_ref)):
        wt[n] = w[0].T
    for t in range(ahead, rows // TILE):
        for c in tile_loads(t):
            c.start()

    def one(t, carry):
        for n in range(STEP // TILE):
            for c in tile_loads(t * (STEP // TILE) + n):
                c.wait()
        at = pl.ds(pl.multiple_of(t * STEP, STEP), STEP)
        k = k_ref[at, :]
        rate = jnp.broadcast_to(rate_ref[:, at], (128, STEP)).T
        rate = jnp.concatenate([rate] * (v_ref.shape[1] // 128), axis=1)
        scaled = (rate * v_ref[at, :].astype(F32)).astype(BF16)
        gate = dot_nt(wt[0], k)
        up = dot_nt(wt[1], k)
        back = dot_nt(wt[2], scaled)
        sig = sigmoid(gate)
        act = gate * sig
        hidden = (act * up).astype(BF16)
        grad_gate = (back * up * (sig + act * (1.0 - sig))).astype(BF16)
        grad_up = (back * act).astype(BF16)
        first = t == 0
        acc[0] = jnp.where(first, 0.0, acc[0]) + dot_nn(grad_gate, k)
        acc[1] = jnp.where(first, 0.0, acc[1]) + dot_nn(grad_up, k)
        acc[2] = jnp.where(first, 0.0, acc[2]) + dot_nn(hidden, scaled)
        return carry

    lax.fori_loop(0, rows // STEP, one, 0)
    z, core = position()
    half, part = keep_ref.shape[1], slice_ref.shape[1]
    mine = pl.multiple_of(core * half, half)
    other = pl.multiple_of((1 - core) * half, half)
    send_ref[...] = acc[:, pl.ds(other, half), :].astype(BF16)
    keep_ref[...] = acc[:, pl.ds(mine, half), :].astype(BF16)
    slice_ref[...] = wt[:, pl.ds(pl.multiple_of(core * half + z * part, part), part), :]


def increments(k, v, rate, w_in, w_up, w_out, z_size):
    rows, hd = k.shape
    fh = w_in.shape[2]
    half, part = fh // 2, fh // 2 // z_size
    anywhere, inside = pl.BlockSpec(memory_space=pl.ANY), pl.BlockSpec(memory_space=pltpu.VMEM)
    return pl.pallas_call(
        increments_kernel,
        in_specs=[anywhere, anywhere, inside, inside, inside, inside],
        out_specs=[inside] * 5,
        out_shape=[pltpu.VMEM((3, half, hd), BF16), pltpu.VMEM((3, half, hd), BF16), pltpu.VMEM((3, part, hd), BF16),
                   pltpu.VMEM((rows, hd), BF16), pltpu.VMEM((rows, hd), BF16)],
        scratch_shapes=[pltpu.VMEM((3, fh, hd), BF16), pltpu.VMEM((3, fh, hd), F32),
                        pltpu.SemaphoreType.DMA((2 * rows // TILE,))],
        cost_estimate=pl.CostEstimate(flops=12 * rows * hd * fh, bytes_accessed=9 << 20,
                                      transcendentals=rows * fh),
        compiler_params=pltpu.CompilerParams(vmem_limit_bytes=45 << 20),
        name="increments",
    )(k, v, rate, w_in, w_up, w_out)


def small_call(kernel, outs, *args):
    return pl.pallas_call(kernel, out_shape=outs, compiler_params=pltpu.CompilerParams(vmem_limit_bytes=8 << 20))(*args)


def pair_sum_kernel(keep_ref, got_ref, *outs):
    count = len(outs)
    part = outs[0].shape[1]
    z, _ = position()
    for d in range(count):
        rows = pl.ds(pl.multiple_of((z + d) % count * part, part), part)
        outs[d][...] = (keep_ref[:, rows, :].astype(F32) + got_ref[:, rows, :].astype(F32)).astype(BF16)


def pair_sum(keep, got, z_size):
    three, half, hd = keep.shape
    return small_call(pair_sum_kernel, [jax.ShapeDtypeStruct((three, half // z_size, hd), BF16)] * z_size,
                      keep, got)


def add_kernel(a_ref, b_ref, o_ref):
    o_ref[...] = (a_ref[...].astype(F32) + b_ref[...].astype(F32)).astype(BF16)


def renorm_kernel(w_ref, *refs):
    parts, out_ref = refs[:-1], refs[-1]
    w = w_ref[...].astype(F32)
    total = parts[0][...].astype(F32)
    for p in parts[1:]:
        total = total + p[...].astype(F32)
    updated = w + total
    size = w.shape[-1]
    before = jnp.sum(w * w, axis=-1, keepdims=True) / size + EPSILON
    after = jnp.sum(updated * updated, axis=-1, keepdims=True) / size + EPSILON
    out_ref[...] = (updated * (jnp.sqrt(before) / jnp.sqrt(after))).astype(BF16)


SIDE = 4
SHIFTS = ((1, 1), (3, 3), (2, 2), (1, 3), (3, 1), (2, 1), (1, 2), (3, 2),
          (2, 3), (2, 0), (0, 2), (1, 0), (0, 1), (3, 0), (0, 3), (0, 0))
GROUPS = (2, 4, 4, 5, 1)
HEAD_AT, TARGET_AT = 0, 1
SOURCE_AT = TARGET_AT + len(SHIFTS)


def shifted(h, dx, dy):
    return (h // SIDE + dx) % SIDE * SIDE + (h + dy) % SIDE


def tail_kernel(k_ref, v_ref, tail_ref, table, sems):
    rows = pl.ds(k_ref.shape[0] - WINDOW, WINDOW)
    copies = [pltpu.make_async_copy(ref.at[rows], tail_ref.at[n], sems.at[n]) for n, ref in enumerate((k_ref, v_ref))]
    for c in copies:
        c.start()
    head = lax.axis_index("head")
    table[HEAD_AT] = head
    for n, (dx, dy) in enumerate(SHIFTS):
        table[TARGET_AT + n] = shifted(head, dx, dy)
        table[SOURCE_AT + n] = shifted(head, SIDE - dx, SIDE - dy)
    for c in copies:
        c.wait()


def tails(k, v):
    hd = k.shape[1]
    return pl.pallas_call(
        tail_kernel,
        in_specs=[pl.BlockSpec(memory_space=pl.ANY)] * 2,
        out_specs=[pl.BlockSpec(memory_space=pltpu.VMEM), pl.BlockSpec(memory_space=pltpu.SMEM)],
        out_shape=[pltpu.VMEM((2, WINDOW, hd), BF16), jax.ShapeDtypeStruct((SOURCE_AT + len(SHIFTS),), jnp.int32)],
        scratch_shapes=[pltpu.SemaphoreType.DMA((2,))],
        compiler_params=pltpu.CompilerParams(vmem_limit_bytes=60 << 20),
        name="tails",
    )(k, v)


def softmax_parts(s, lo, scale):
    tq, span = s.shape[0], s.shape[1]
    row = lax.broadcasted_iota(jnp.int32, (tq, tq), 0)
    col = lax.broadcasted_iota(jnp.int32, (tq, tq), 1)
    if lo is not None:
        s = jnp.where(lax.broadcasted_iota(jnp.int32, (tq, span), 1) >= lo, s, -1e30)
    parts = [jnp.where(col > row, s[:, :tq], -1e30), s[:, tq:WINDOW], jnp.where(col <= row, s[:, WINDOW:], -1e30)]
    top = jnp.maximum(jnp.max(jnp.maximum(parts[0], parts[2]), axis=1, keepdims=True),
                      jnp.max(parts[1], axis=1, keepdims=True)) * scale
    p = jnp.concatenate([jnp.exp2(x * scale - top) for x in parts], axis=1)
    return p.astype(BF16), 1.0 / jnp.sum(p, axis=1, keepdims=True)


def attend(q_rows, o_store, key_rows, value_rows, lo, count, scale):
    scores = dot_nt(q_rows(0), key_rows(0))
    for n in range(count):
        ahead = dot_nt(q_rows(n + 1), key_rows(n + 1)) if n + 1 < count else None
        p, inverse = softmax_parts(scores, None if lo is None else lo(n), scale)
        o_store(n, (dot_nn(p, value_rows(n)) * inverse).astype(BF16))
        scores = ahead


def attention_own_kernel(q_ref, k_ref, v_ref, *refs, tq, per, start, stop, scale):
    o_ref = refs[-1]

    def one(t, carry):
        first = start + t * per * tq

        def rows(ref, size, back):
            return lambda n: ref[pl.ds(pl.multiple_of(first + n * tq - back, tq), size), :]

        def store(n, x):
            o_ref[pl.ds(pl.multiple_of(first + n * tq, tq), tq), :] = x

        attend(rows(q_ref, tq, 0), store, rows(k_ref, WINDOW + tq, WINDOW), rows(v_ref, WINDOW + tq, WINDOW),
               None, per, scale)
        return carry

    lax.fori_loop(0, (stop - start) // (per * tq), one, 0)


def attention_first_kernel(q_ref, b_ref, k_ref, v_ref, _, o_ref, *, tq, scale):
    z, core = position()
    limit = jnp.where(z + core == 0, WINDOW, 0)

    def window(which, ref):
        return lambda n: jnp.concatenate([b_ref[which, n * tq:, :], ref[:(n + 1) * tq, :]], axis=0)

    def store(n, x):
        o_ref[n * tq:(n + 1) * tq, :] = x

    attend(lambda n: q_ref[n * tq:(n + 1) * tq, :], store, window(0, k_ref), window(1, v_ref),
           lambda n: limit - n * tq, WINDOW // tq, scale)


INSIDE = pl.BlockSpec(memory_space=pltpu.VMEM)


def attention_own(q, k, v, start, stop, attended=None, tq=256, per=2):
    rows, hd = q.shape
    into = [] if attended is None else [attended]
    return pl.pallas_call(
        functools.partial(attention_own_kernel, tq=tq, per=per, start=start, stop=stop, scale=hd ** -0.5 * LOG2E),
        in_specs=[INSIDE] * (3 + len(into)),
        out_specs=INSIDE,
        out_shape=pltpu.VMEM((rows, hd), BF16),
        input_output_aliases={3: 0} if into else {},
        cost_estimate=pl.CostEstimate(flops=4 * (stop - start) * (WINDOW + tq) * hd,
                                      bytes_accessed=8 << 20, transcendentals=(stop - start) * WINDOW),
        compiler_params=pltpu.CompilerParams(vmem_limit_bytes=14 << 20),
        name="attention_own",
    )(q, k, v, *into)


def attention_first(q, before, k, v, attended, tq=256):
    hd = q.shape[1]
    return pl.pallas_call(
        functools.partial(attention_first_kernel, tq=tq, scale=hd ** -0.5 * LOG2E),
        in_specs=[INSIDE] * 5,
        out_specs=INSIDE,
        out_shape=pltpu.VMEM(attended.shape, BF16),
        input_output_aliases={4: 0},
        cost_estimate=pl.CostEstimate(flops=4 * WINDOW * (WINDOW + tq) * hd,
                                      bytes_accessed=6 << 20, transcendentals=WINDOW * WINDOW),
        compiler_params=pltpu.CompilerParams(vmem_limit_bytes=18 << 20),
        name="attention_first",
    )(q, before, k, v, attended)


EXTRA = 8
LANES = 256


def apply_kernel(table, q_ref, attended_ref, gate_ref, gain_ref, *refs, count, n_pieces, at):
    weights, outs = refs[:n_pieces], refs[n_pieces:]
    if n_pieces > 1:
        wt, start = outs[-1], 0
        for p in weights:
            wt[:, start:start + p.shape[1], :] = p[...]
            start += p.shape[1]
    else:
        wt = weights[0]
    share, hd = q_ref.shape[1:]
    targets = [table[TARGET_AT + at + n] for n in range(count)]
    gain = gain_ref[:, pl.ds(pl.multiple_of(table[HEAD_AT] * hd, hd), hd)]
    q = jnp.concatenate([q_ref[t] for t in targets], axis=0)
    hidden = (silu(dot_nt(q, wt[0])) * dot_nt(q, wt[1])).astype(BF16)
    fast = dot_nn(hidden, wt[2])
    for n, t in enumerate(targets):
        rows = slice(n * share, (n + 1) * share)
        head = (attended_ref[t].astype(F32) + fast[rows]).astype(BF16).astype(F32)
        squares = jnp.sum(head * head, axis=1, keepdims=True)
        y = outs[n]
        y[:share, :] = (head * (gain * silu(gate_ref[t].astype(F32)))).astype(BF16)
        column = jnp.concatenate([squares, jnp.zeros((LANES - share, 1), F32)], axis=0)
        line = jnp.broadcast_to(column, (LANES, 128)).T[:EXTRA, :]
        high = line.astype(BF16)
        low = (line - high.astype(F32)).astype(BF16)
        y[share:, :LANES] = high
        y[share:, LANES:] = low


def applied(table, q, attended, out_gate, gain, weights, n_head, at, count):
    rows, hd = q.shape
    share = rows // n_head
    fh = sum(p.shape[1] for p in weights)
    blocks = [a.reshape(n_head, share, hd) for a in (q, attended, out_gate)]
    inside = pl.BlockSpec(memory_space=pltpu.VMEM)
    outs = [pltpu.VMEM((share + EXTRA, hd), BF16)] * count
    if len(weights) > 1:
        outs.append(pltpu.VMEM((3, fh, hd), BF16))
    return pl.pallas_call(
        functools.partial(apply_kernel, count=count, n_pieces=len(weights), at=at),
        in_specs=[pl.BlockSpec(memory_space=pltpu.SMEM)] + [inside] * (4 + len(weights)),
        out_specs=[inside] * len(outs),
        out_shape=outs,
        cost_estimate=pl.CostEstimate(flops=6 * count * share * hd * fh, bytes_accessed=count << 20,
                                      transcendentals=2 * count * share * fh),
        compiler_params=pltpu.CompilerParams(vmem_limit_bytes=18 << 20),
        name="apply_fast",
    )(table, *blocks, gain, *weights)


def scale_kernel(table, *refs):
    count = (len(refs) - 2) // 1 - 1
    y_refs, (o_ref, buf, sems) = refs[:count], refs[count:]
    share, width = buf.shape[1:]
    s = y_refs[0][share:, :].astype(F32)
    for y in y_refs[1:]:
        s = s + y[share:, :].astype(F32)
    line = s[:, :LANES] + s[:, LANES:]
    r = lax.rsqrt(line / (count * width) + EPSILON)
    r = jnp.concatenate([r] * (128 // EXTRA), axis=0).T[:share, :]
    r = jnp.concatenate([r] * (width // 128), axis=1)
    copies = []
    for n in range(count):
        buf[n] = (y_refs[n][:share, :].astype(F32) * r).astype(BF16)
        columns = pl.ds(pl.multiple_of(table[SOURCE_AT + n] * width, width), width)
        copies.append(pltpu.make_async_copy(buf.at[n], o_ref.at[:, columns], sems.at[n]))
        copies[-1].start()
    for c in copies:
        c.wait()


def scaled_rows(table, parts):
    rows, hd = parts[0].shape
    share, count = rows - EXTRA, len(parts)
    return pl.pallas_call(
        scale_kernel,
        in_specs=[pl.BlockSpec(memory_space=pltpu.SMEM)] + [pl.BlockSpec(memory_space=pltpu.VMEM)] * count,
        out_specs=pl.BlockSpec(memory_space=pl.ANY),
        out_shape=jax.ShapeDtypeStruct((share, count * hd), BF16),
        scratch_shapes=[pltpu.VMEM((count, share, hd), BF16), pltpu.SemaphoreType.DMA((count,))],
        compiler_params=pltpu.CompilerParams(vmem_limit_bytes=12 << 20),
        name="scale_rows",
    )(table, *parts)


def layer(queries, key_vectors, value_vectors, step_sizes, w_in, w_up, w_out, out_gate, norm_gain):
    rows, _ = queries.shape
    n_ctx, n_head = lax.axis_size("ctx"), lax.axis_size("head")
    z_size = n_ctx // 2
    tied = lax.optimization_barrier

    def along_z(x, d):
        return lax.ppermute(x, "ctx", [(i, ((i // 2 + d) % z_size) * 2 + i % 2) for i in range(n_ctx)])

    def swapped(x):
        return lax.ppermute(x, "ctx", [(i, i ^ 1) for i in range(n_ctx)])

    tail, table = tails(key_vectors, value_vectors)
    before = lax.ppermute(tail, "ctx", [(i, i + 1) for i in range(n_ctx - 1)])
    early = [pltpu.with_memory_space_constraint(x, pltpu.VMEM) for x in (step_sizes, w_in, w_up, w_out)]
    keep, send, w_slice, keys, values = increments(key_vectors, value_vectors, *early, z_size)

    order = sorted(range(1, z_size), key=lambda d: -min(d, z_size - d))
    parts = pair_sum(keep, swapped(send), z_size)
    below = z_size - 1
    from_far, from_below = along_z(parts[2], below), along_z(parts[1], 1)
    q, own = tied((queries, parts[0]))
    half = rows - WINDOW
    attended = attention_own(q, keys, values, WINDOW, half)
    attended, from_far = tied((attended, from_far))
    both = small_call(add_kernel, jax.ShapeDtypeStruct(own.shape, BF16), parts[below], from_far)
    from_above = along_z(both, below)
    q, own, _ = tied((queries, own, both))
    attended = attention_own(q, keys, values, half, rows, attended)
    attended, from_below, from_above = tied((attended, from_below, from_above))
    piece = small_call(renorm_kernel, jax.ShapeDtypeStruct(own.shape, BF16),
                       w_slice, own, from_below, from_above)
    rest = [along_z(piece, d) for d in order]
    q, piece = tied((queries, piece))
    attended = attention_first(q, before, keys, values, attended)
    attended, rest = tied((attended, rest))
    chip = [piece] + rest
    other = [swapped(p) for p in chip]

    weights, gain = chip + other, norm_gain.reshape(1, -1)
    parts, at = [], 0
    for count in GROUPS:
        outs = applied(table, queries, attended, out_gate, gain, weights, n_head, at, count)
        if len(outs) > count:
            weights = outs[count:]
        for y, (dx, dy) in zip(outs, SHIFTS[at:at + count]):
            if dx or dy:
                y = lax.ppermute(y, "head", [(h, shifted(h, dx, dy)) for h in range(n_head)])
            parts.append(y)
        at += count
    return scaled_rows(table, parts)


def solution(mesh):
    return jax.shard_map(
        layer,
        mesh=mesh,
        in_specs=(
            P("ctx", "head"), P("ctx", "head"), P("ctx", "head"), P("head", "ctx"),
            P("head", None, None), P("head", None, None), P("head", None, None),
            P("ctx", "head"), P(),
        ),
        out_specs=P(("ctx", "head"), None),
        check_vma=False,
    )
```

```python
import functools

import jax
import jax.numpy as jnp
from jax import lax
from jax.experimental import pallas as pl
from jax.experimental.pallas import tpu as pltpu
from jax.sharding import PartitionSpec as P


WINDOW = 1024
EPSILON = 1e-06
LOG2E = 1.4426950408889634


F32 = jnp.float32
BF16 = jnp.bfloat16
NT = (((1,), (1,)), ((), ()))


def sigmoid(x):
    return 0.5 * jnp.tanh(0.5 * x) + 0.5


def silu(x):
    half = 0.5 * x
    return half * jnp.tanh(half) + half


def dot_nt(a, b):
    return lax.dot_general(a, b, NT, preferred_element_type=F32)


def dot_nn(a, b):
    return jnp.dot(a, b, preferred_element_type=F32)


def position():
    ctx = lax.axis_index("ctx")
    return ctx // 2, ctx % 2


TILE = 512


STEP = 1024


def increments_kernel(k_hbm, v_hbm, rate_ref, wi_ref, wu_ref, wo_ref,
                      keep_ref, send_ref, slice_ref, k_ref, v_ref, wt, acc, sems):
    rows = k_ref.shape[0]

    def tile_loads(t):
        at = pl.ds(pl.multiple_of(t * TILE, TILE), TILE)
        return (pltpu.make_async_copy(k_hbm.at[at], k_ref.at[at], sems.at[2 * t]),
                pltpu.make_async_copy(v_hbm.at[at], v_ref.at[at], sems.at[2 * t + 1]))

    ahead = STEP // TILE
    for t in range(ahead):
        for c in tile_loads(t):
            c.start()
    for n, w in enumerate((wi_ref, wu_ref, wo_ref)):
        wt[n] = w[0].T
    for t in range(ahead, rows // TILE):
        for c in tile_loads(t):
            c.start()

    def one(t, carry):
        for n in range(STEP // TILE):
            for c in tile_loads(t * (STEP // TILE) + n):
                c.wait()
        at = pl.ds(pl.multiple_of(t * STEP, STEP), STEP)
        k = k_ref[at, :]
        rate = jnp.broadcast_to(rate_ref[:, at], (128, STEP)).T
        rate = jnp.concatenate([rate] * (v_ref.shape[1] // 128), axis=1)
        scaled = (rate * v_ref[at, :].astype(F32)).astype(BF16)
        gate = dot_nt(wt[0], k)
        up = dot_nt(wt[1], k)
        back = dot_nt(wt[2], scaled)
        sig = sigmoid(gate)
        act = gate * sig
        hidden = (act * up).astype(BF16)
        grad_gate = (back * up * (sig + act * (1.0 - sig))).astype(BF16)
        grad_up = (back * act).astype(BF16)
        first = t == 0
        acc[0] = jnp.where(first, 0.0, acc[0]) + dot_nn(grad_gate, k)
        acc[1] = jnp.where(first, 0.0, acc[1]) + dot_nn(grad_up, k)
        acc[2] = jnp.where(first, 0.0, acc[2]) + dot_nn(hidden, scaled)
        return carry

    lax.fori_loop(0, rows // STEP, one, 0)
    z, core = position()
    half, part = keep_ref.shape[1], slice_ref.shape[1]
    mine = pl.multiple_of(core * half, half)
    other = pl.multiple_of((1 - core) * half, half)
    send_ref[...] = acc[:, pl.ds(other, half), :].astype(BF16)
    keep_ref[...] = acc[:, pl.ds(mine, half), :].astype(BF16)
    slice_ref[...] = wt[:, pl.ds(pl.multiple_of(core * half + z * part, part), part), :]


def increments(k, v, rate, w_in, w_up, w_out, z_size):
    rows, hd = k.shape
    fh = w_in.shape[2]
    half, part = fh // 2, fh // 2 // z_size
    anywhere, inside = pl.BlockSpec(memory_space=pl.ANY), pl.BlockSpec(memory_space=pltpu.VMEM)
    return pl.pallas_call(
        increments_kernel,
        in_specs=[anywhere, anywhere, inside, inside, inside, inside],
        out_specs=[inside] * 5,
        out_shape=[pltpu.VMEM((3, half, hd), BF16), pltpu.VMEM((3, half, hd), BF16), pltpu.VMEM((3, part, hd), BF16),
                   pltpu.VMEM((rows, hd), BF16), pltpu.VMEM((rows, hd), BF16)],
        scratch_shapes=[pltpu.VMEM((3, fh, hd), BF16), pltpu.VMEM((3, fh, hd), F32),
                        pltpu.SemaphoreType.DMA((2 * rows // TILE,))],
        cost_estimate=pl.CostEstimate(flops=12 * rows * hd * fh, bytes_accessed=9 << 20,
                                      transcendentals=rows * fh),
        compiler_params=pltpu.CompilerParams(vmem_limit_bytes=45 << 20),
        name="increments",
    )(k, v, rate, w_in, w_up, w_out)


def small_call(kernel, outs, *args):
    return pl.pallas_call(kernel, out_shape=outs, compiler_params=pltpu.CompilerParams(vmem_limit_bytes=8 << 20))(*args)


def pair_sum_kernel(keep_ref, got_ref, *outs):
    count = len(outs)
    part = outs[0].shape[1]
    z, _ = position()
    for d in range(count):
        rows = pl.ds(pl.multiple_of((z + d) % count * part, part), part)
        outs[d][...] = (keep_ref[:, rows, :].astype(F32) + got_ref[:, rows, :].astype(F32)).astype(BF16)


def pair_sum(keep, got, z_size):
    three, half, hd = keep.shape
    return small_call(pair_sum_kernel, [jax.ShapeDtypeStruct((three, half // z_size, hd), BF16)] * z_size,
                      keep, got)


def add_kernel(a_ref, b_ref, o_ref):
    o_ref[...] = (a_ref[...].astype(F32) + b_ref[...].astype(F32)).astype(BF16)


def renorm_kernel(w_ref, *refs):
    parts, out_ref = refs[:-1], refs[-1]
    w = w_ref[...].astype(F32)
    total = parts[0][...].astype(F32)
    for p in parts[1:]:
        total = total + p[...].astype(F32)
    updated = w + total
    size = w.shape[-1]
    before = jnp.sum(w * w, axis=-1, keepdims=True) / size + EPSILON
    after = jnp.sum(updated * updated, axis=-1, keepdims=True) / size + EPSILON
    out_ref[...] = (updated * (jnp.sqrt(before) / jnp.sqrt(after))).astype(BF16)


SIDE = 4
SHIFTS = ((1, 1), (3, 3), (2, 2), (1, 3), (3, 1), (2, 1), (1, 2), (3, 2),
          (2, 3), (2, 0), (0, 2), (1, 0), (0, 1), (3, 0), (0, 3), (0, 0))
GROUPS = (2, 4, 4, 5, 1)
HEAD_AT, TARGET_AT = 0, 1
SOURCE_AT = TARGET_AT + len(SHIFTS)


def shifted(h, dx, dy):
    return (h // SIDE + dx) % SIDE * SIDE + (h + dy) % SIDE


def tail_kernel(k_ref, v_ref, tail_ref, table, sems):
    rows = pl.ds(k_ref.shape[0] - WINDOW, WINDOW)
    copies = [pltpu.make_async_copy(ref.at[rows], tail_ref.at[n], sems.at[n]) for n, ref in enumerate((k_ref, v_ref))]
    for c in copies:
        c.start()
    head = lax.axis_index("head")
    _, core = position()
    table[HEAD_AT] = head
    for n, (dx, dy) in enumerate(SHIFTS):
        forth, back = shifted(head, dx, dy), shifted(head, SIDE - dx, SIDE - dy)
        table[TARGET_AT + n] = jnp.where(core == 0, forth, back)
        table[SOURCE_AT + n] = jnp.where(core == 0, back, forth)
    for c in copies:
        c.wait()


def tails(k, v):
    hd = k.shape[1]
    return pl.pallas_call(
        tail_kernel,
        in_specs=[pl.BlockSpec(memory_space=pl.ANY)] * 2,
        out_specs=[pl.BlockSpec(memory_space=pltpu.VMEM), pl.BlockSpec(memory_space=pltpu.SMEM)],
        out_shape=[pltpu.VMEM((2, WINDOW, hd), BF16), jax.ShapeDtypeStruct((SOURCE_AT + len(SHIFTS),), jnp.int32)],
        scratch_shapes=[pltpu.SemaphoreType.DMA((2,))],
        compiler_params=pltpu.CompilerParams(vmem_limit_bytes=60 << 20),
        name="tails",
    )(k, v)


def softmax_parts(s, lo, scale):
    tq, span = s.shape[0], s.shape[1]
    row = lax.broadcasted_iota(jnp.int32, (tq, tq), 0)
    col = lax.broadcasted_iota(jnp.int32, (tq, tq), 1)
    if lo is not None:
        s = jnp.where(lax.broadcasted_iota(jnp.int32, (tq, span), 1) >= lo, s, -1e30)
    parts = [jnp.where(col > row, s[:, :tq], -1e30), s[:, tq:WINDOW], jnp.where(col <= row, s[:, WINDOW:], -1e30)]
    top = jnp.maximum(jnp.max(jnp.maximum(parts[0], parts[2]), axis=1, keepdims=True),
                      jnp.max(parts[1], axis=1, keepdims=True)) * scale
    p = jnp.concatenate([jnp.exp2(x * scale - top) for x in parts], axis=1)
    return p.astype(BF16), 1.0 / jnp.sum(p, axis=1, keepdims=True)


def attend(q_rows, o_store, key_rows, value_rows, lo, count, scale):
    scores = dot_nt(q_rows(0), key_rows(0))
    for n in range(count):
        ahead = dot_nt(q_rows(n + 1), key_rows(n + 1)) if n + 1 < count else None
        p, inverse = softmax_parts(scores, None if lo is None else lo(n), scale)
        o_store(n, (dot_nn(p, value_rows(n)) * inverse).astype(BF16))
        scores = ahead


def attention_own_kernel(q_ref, k_ref, v_ref, *refs, tq, per, start, stop, scale):
    o_ref = refs[-1]

    def one(t, carry):
        first = start + t * per * tq

        def rows(ref, size, back):
            return lambda n: ref[pl.ds(pl.multiple_of(first + n * tq - back, tq), size), :]

        def store(n, x):
            o_ref[pl.ds(pl.multiple_of(first + n * tq, tq), tq), :] = x

        attend(rows(q_ref, tq, 0), store, rows(k_ref, WINDOW + tq, WINDOW), rows(v_ref, WINDOW + tq, WINDOW),
               None, per, scale)
        return carry

    lax.fori_loop(0, (stop - start) // (per * tq), one, 0)


def attention_first_kernel(q_ref, b_ref, k_ref, v_ref, _, o_ref, *, tq, scale):
    z, core = position()
    limit = jnp.where(z + core == 0, WINDOW, 0)

    def window(which, ref):
        return lambda n: jnp.concatenate([b_ref[which, n * tq:, :], ref[:(n + 1) * tq, :]], axis=0)

    def store(n, x):
        o_ref[n * tq:(n + 1) * tq, :] = x

    attend(lambda n: q_ref[n * tq:(n + 1) * tq, :], store, window(0, k_ref), window(1, v_ref),
           lambda n: limit - n * tq, WINDOW // tq, scale)


INSIDE = pl.BlockSpec(memory_space=pltpu.VMEM)


def attention_own(q, k, v, start, stop, attended=None, tq=256, per=2):
    rows, hd = q.shape
    into = [] if attended is None else [attended]
    return pl.pallas_call(
        functools.partial(attention_own_kernel, tq=tq, per=per, start=start, stop=stop, scale=hd ** -0.5 * LOG2E),
        in_specs=[INSIDE] * (3 + len(into)),
        out_specs=INSIDE,
        out_shape=pltpu.VMEM((rows, hd), BF16),
        input_output_aliases={3: 0} if into else {},
        cost_estimate=pl.CostEstimate(flops=4 * (stop - start) * (WINDOW + tq) * hd,
                                      bytes_accessed=8 << 20, transcendentals=(stop - start) * WINDOW),
        compiler_params=pltpu.CompilerParams(vmem_limit_bytes=14 << 20),
        name="attention_own",
    )(q, k, v, *into)


def attention_first(q, before, k, v, attended, tq=256):
    hd = q.shape[1]
    return pl.pallas_call(
        functools.partial(attention_first_kernel, tq=tq, scale=hd ** -0.5 * LOG2E),
        in_specs=[INSIDE] * 5,
        out_specs=INSIDE,
        out_shape=pltpu.VMEM(attended.shape, BF16),
        input_output_aliases={4: 0},
        cost_estimate=pl.CostEstimate(flops=4 * WINDOW * (WINDOW + tq) * hd,
                                      bytes_accessed=6 << 20, transcendentals=WINDOW * WINDOW),
        compiler_params=pltpu.CompilerParams(vmem_limit_bytes=18 << 20),
        name="attention_first",
    )(q, before, k, v, attended)


EXTRA = 8
LANES = 256


def apply_kernel(table, q_ref, attended_ref, gate_ref, gain_ref, *refs, count, n_pieces, at):
    weights, outs = refs[:n_pieces], refs[n_pieces:]
    if n_pieces > 1:
        wt, start = outs[-1], 0
        for p in weights:
            wt[:, start:start + p.shape[1], :] = p[...]
            start += p.shape[1]
    else:
        wt = weights[0]
    share, hd = q_ref.shape[1:]
    targets = [table[TARGET_AT + at + n] for n in range(count)]
    gain = gain_ref[:, pl.ds(pl.multiple_of(table[HEAD_AT] * hd, hd), hd)]
    q = jnp.concatenate([q_ref[t] for t in targets], axis=0)
    hidden = (silu(dot_nt(q, wt[0])) * dot_nt(q, wt[1])).astype(BF16)
    fast = dot_nn(hidden, wt[2])
    for n, t in enumerate(targets):
        rows = slice(n * share, (n + 1) * share)
        head = (attended_ref[t].astype(F32) + fast[rows]).astype(BF16).astype(F32)
        squares = jnp.sum(head * head, axis=1, keepdims=True)
        y = outs[n]
        y[:share, :] = (head * (gain * silu(gate_ref[t].astype(F32)))).astype(BF16)
        column = jnp.concatenate([squares, jnp.zeros((LANES - share, 1), F32)], axis=0)
        line = jnp.broadcast_to(column, (LANES, 128)).T[:EXTRA, :]
        high = line.astype(BF16)
        low = (line - high.astype(F32)).astype(BF16)
        y[share:, :LANES] = high
        y[share:, LANES:] = low


def applied(table, q, attended, out_gate, gain, weights, n_head, at, count):
    rows, hd = q.shape
    share = rows // n_head
    fh = sum(p.shape[1] for p in weights)
    blocks = [a.reshape(n_head, share, hd) for a in (q, attended, out_gate)]
    inside = pl.BlockSpec(memory_space=pltpu.VMEM)
    outs = [pltpu.VMEM((share + EXTRA, hd), BF16)] * count
    if len(weights) > 1:
        outs.append(pltpu.VMEM((3, fh, hd), BF16))
    return pl.pallas_call(
        functools.partial(apply_kernel, count=count, n_pieces=len(weights), at=at),
        in_specs=[pl.BlockSpec(memory_space=pltpu.SMEM)] + [inside] * (4 + len(weights)),
        out_specs=[inside] * len(outs),
        out_shape=outs,
        cost_estimate=pl.CostEstimate(flops=6 * count * share * hd * fh, bytes_accessed=count << 20,
                                      transcendentals=2 * count * share * fh),
        compiler_params=pltpu.CompilerParams(vmem_limit_bytes=18 << 20),
        name="apply_fast",
    )(table, *blocks, gain, *weights)


def scale_kernel(table, *refs):
    count = (len(refs) - 2) // 1 - 1
    y_refs, (o_ref, buf, sems) = refs[:count], refs[count:]
    share, width = buf.shape[1:]
    s = y_refs[0][share:, :].astype(F32)
    for y in y_refs[1:]:
        s = s + y[share:, :].astype(F32)
    line = s[:, :LANES] + s[:, LANES:]
    r = lax.rsqrt(line / (count * width) + EPSILON)
    r = jnp.concatenate([r] * (128 // EXTRA), axis=0).T[:share, :]
    r = jnp.concatenate([r] * (width // 128), axis=1)
    copies = []
    for n in range(count):
        buf[n] = (y_refs[n][:share, :].astype(F32) * r).astype(BF16)
        columns = pl.ds(pl.multiple_of(table[SOURCE_AT + n] * width, width), width)
        copies.append(pltpu.make_async_copy(buf.at[n], o_ref.at[:, columns], sems.at[n]))
        copies[-1].start()
    for c in copies:
        c.wait()


def scaled_rows(table, parts):
    rows, hd = parts[0].shape
    share, count = rows - EXTRA, len(parts)
    return pl.pallas_call(
        scale_kernel,
        in_specs=[pl.BlockSpec(memory_space=pltpu.SMEM)] + [pl.BlockSpec(memory_space=pltpu.VMEM)] * count,
        out_specs=pl.BlockSpec(memory_space=pl.ANY),
        out_shape=jax.ShapeDtypeStruct((share, count * hd), BF16),
        scratch_shapes=[pltpu.VMEM((count, share, hd), BF16), pltpu.SemaphoreType.DMA((count,))],
        compiler_params=pltpu.CompilerParams(vmem_limit_bytes=12 << 20),
        name="scale_rows",
    )(table, *parts)


def layer(queries, key_vectors, value_vectors, step_sizes, w_in, w_up, w_out, out_gate, norm_gain):
    rows, _ = queries.shape
    n_ctx, n_head = lax.axis_size("ctx"), lax.axis_size("head")
    z_size = n_ctx // 2
    tied = lax.optimization_barrier

    def along_z(x, d):
        return lax.ppermute(x, "ctx", [(i, ((i // 2 + d) % z_size) * 2 + i % 2) for i in range(n_ctx)])

    def swapped(x):
        return lax.ppermute(x, "ctx", [(i, i ^ 1) for i in range(n_ctx)])

    tail, table = tails(key_vectors, value_vectors)
    before = lax.ppermute(tail, "ctx", [(i, i + 1) for i in range(n_ctx - 1)])
    early = [pltpu.with_memory_space_constraint(x, pltpu.VMEM) for x in (step_sizes, w_in, w_up, w_out)]
    keep, send, w_slice, keys, values = increments(key_vectors, value_vectors, *early, z_size)

    order = sorted(range(1, z_size), key=lambda d: -min(d, z_size - d))
    parts = pair_sum(keep, swapped(send), z_size)
    below = z_size - 1
    from_far, from_below = along_z(parts[2], below), along_z(parts[1], 1)
    q, own = tied((queries, parts[0]))
    half = rows - WINDOW
    attended = attention_own(q, keys, values, WINDOW, half)
    attended, from_far = tied((attended, from_far))
    both = small_call(add_kernel, jax.ShapeDtypeStruct(own.shape, BF16), parts[below], from_far)
    from_above = along_z(both, below)
    q, own, _ = tied((queries, own, both))
    attended = attention_own(q, keys, values, half, rows, attended)
    attended, from_below, from_above = tied((attended, from_below, from_above))
    piece = small_call(renorm_kernel, jax.ShapeDtypeStruct(own.shape, BF16),
                       w_slice, own, from_below, from_above)
    rest = [along_z(piece, d) for d in order]
    q, piece = tied((queries, piece))
    attended = attention_first(q, before, keys, values, attended)
    attended, rest = tied((attended, rest))
    chip = [piece] + rest
    other = [swapped(p) for p in chip]

    weights, gain = chip + other, norm_gain.reshape(1, -1)
    parts, at = [], 0
    for count in GROUPS:
        outs = applied(table, queries, attended, out_gate, gain, weights, n_head, at, count)
        if len(outs) > count:
            weights = outs[count:]
        for y, (dx, dy) in zip(outs, SHIFTS[at:at + count]):
            if dx or dy:
                ways = ((dx, dy), (SIDE - dx, SIDE - dy))
                y = lax.ppermute(y, ("ctx", "head"), [
                    (c * n_head + h, c * n_head + shifted(h, *ways[c % 2])) for c in range(n_ctx) for h in range(n_head)])
            parts.append(y)
        at += count
    return scaled_rows(table, parts)


def solution(mesh):
    return jax.shard_map(
        layer,
        mesh=mesh,
        in_specs=(
            P("ctx", "head"), P("ctx", "head"), P("ctx", "head"), P("head", "ctx"),
            P("head", None, None), P("head", None, None), P("head", None, None),
            P("ctx", "head"), P(),
        ),
        out_specs=P(("ctx", "head"), None),
        check_vma=False,
    )
```

```python
import functools

import jax
import jax.numpy as jnp
from jax import lax
from jax.experimental import pallas as pl
from jax.experimental.pallas import tpu as pltpu
from jax.sharding import PartitionSpec as P


WINDOW = 1024
EPSILON = 1e-06
LOG2E = 1.4426950408889634


F32 = jnp.float32
BF16 = jnp.bfloat16
NT = (((1,), (1,)), ((), ()))


def sigmoid(x):
    return 0.5 * jnp.tanh(0.5 * x) + 0.5


def silu(x):
    half = 0.5 * x
    return half * jnp.tanh(half) + half


def dot_nt(a, b):
    return lax.dot_general(a, b, NT, preferred_element_type=F32)


def dot_nn(a, b):
    return jnp.dot(a, b, preferred_element_type=F32)


def position():
    ctx = lax.axis_index("ctx")
    return ctx // 2, ctx % 2


TILE = 512


STEP = 1024


def increments_kernel(k_hbm, v_hbm, rate_ref, wi_ref, wu_ref, wo_ref,
                      keep_ref, send_ref, slice_ref, k_ref, v_ref, wt, acc, sems):
    rows = k_ref.shape[0]

    def tile_loads(t):
        at = pl.ds(pl.multiple_of(t * TILE, TILE), TILE)
        return (pltpu.make_async_copy(k_hbm.at[at], k_ref.at[at], sems.at[2 * t]),
                pltpu.make_async_copy(v_hbm.at[at], v_ref.at[at], sems.at[2 * t + 1]))

    ahead = STEP // TILE
    for t in range(ahead):
        for c in tile_loads(t):
            c.start()
    for n, w in enumerate((wi_ref, wu_ref, wo_ref)):
        wt[n] = w[0].T
    for t in range(ahead, rows // TILE):
        for c in tile_loads(t):
            c.start()

    def one(t, carry):
        for n in range(STEP // TILE):
            for c in tile_loads(t * (STEP // TILE) + n):
                c.wait()
        at = pl.ds(pl.multiple_of(t * STEP, STEP), STEP)
        k = k_ref[at, :]
        rate = jnp.broadcast_to(rate_ref[:, at], (128, STEP)).T
        rate = jnp.concatenate([rate] * (v_ref.shape[1] // 128), axis=1)
        scaled = (rate * v_ref[at, :].astype(F32)).astype(BF16)
        gate = dot_nt(wt[0], k)
        up = dot_nt(wt[1], k)
        back = dot_nt(wt[2], scaled)
        sig = sigmoid(gate)
        act = gate * sig
        hidden = (act * up).astype(BF16)
        grad_gate = (back * up * (sig + act * (1.0 - sig))).astype(BF16)
        grad_up = (back * act).astype(BF16)
        first = t == 0
        acc[0] = jnp.where(first, 0.0, acc[0]) + dot_nn(grad_gate, k)
        acc[1] = jnp.where(first, 0.0, acc[1]) + dot_nn(grad_up, k)
        acc[2] = jnp.where(first, 0.0, acc[2]) + dot_nn(hidden, scaled)
        return carry

    lax.fori_loop(0, rows // STEP, one, 0)
    z, core = position()
    half, part = keep_ref.shape[1], slice_ref.shape[1]
    mine = pl.multiple_of(core * half, half)
    other = pl.multiple_of((1 - core) * half, half)
    send_ref[...] = acc[:, pl.ds(other, half), :].astype(BF16)
    keep_ref[...] = acc[:, pl.ds(mine, half), :].astype(BF16)
    slice_ref[...] = wt[:, pl.ds(pl.multiple_of(core * half + z * part, part), part), :]


def increments(k, v, rate, w_in, w_up, w_out, z_size):
    rows, hd = k.shape
    fh = w_in.shape[2]
    half, part = fh // 2, fh // 2 // z_size
    anywhere, inside = pl.BlockSpec(memory_space=pl.ANY), pl.BlockSpec(memory_space=pltpu.VMEM)
    return pl.pallas_call(
        increments_kernel,
        in_specs=[anywhere, anywhere, inside, inside, inside, inside],
        out_specs=[inside] * 5,
        out_shape=[pltpu.VMEM((3, half, hd), BF16), pltpu.VMEM((3, half, hd), BF16), pltpu.VMEM((3, part, hd), BF16),
                   pltpu.VMEM((rows, hd), BF16), pltpu.VMEM((rows, hd), BF16)],
        scratch_shapes=[pltpu.VMEM((3, fh, hd), BF16), pltpu.VMEM((3, fh, hd), F32),
                        pltpu.SemaphoreType.DMA((2 * rows // TILE,))],
        cost_estimate=pl.CostEstimate(flops=12 * rows * hd * fh, bytes_accessed=9 << 20,
                                      transcendentals=rows * fh),
        compiler_params=pltpu.CompilerParams(vmem_limit_bytes=45 << 20),
        name="increments",
    )(k, v, rate, w_in, w_up, w_out)


def small_call(kernel, outs, *args):
    return pl.pallas_call(kernel, out_shape=outs, compiler_params=pltpu.CompilerParams(vmem_limit_bytes=8 << 20))(*args)


def pair_sum_kernel(keep_ref, got_ref, *outs):
    count = len(outs)
    part = outs[0].shape[1]
    z, _ = position()
    for d in range(count):
        rows = pl.ds(pl.multiple_of((z + d) % count * part, part), part)
        outs[d][...] = (keep_ref[:, rows, :].astype(F32) + got_ref[:, rows, :].astype(F32)).astype(BF16)


def pair_sum(keep, got, z_size):
    three, half, hd = keep.shape
    return small_call(pair_sum_kernel, [jax.ShapeDtypeStruct((three, half // z_size, hd), BF16)] * z_size,
                      keep, got)


def add_kernel(a_ref, b_ref, o_ref):
    o_ref[...] = (a_ref[...].astype(F32) + b_ref[...].astype(F32)).astype(BF16)


def renorm_kernel(w_ref, *refs):
    parts, out_ref = refs[:-1], refs[-1]
    w = w_ref[...].astype(F32)
    total = parts[0][...].astype(F32)
    for p in parts[1:]:
        total = total + p[...].astype(F32)
    updated = w + total
    size = w.shape[-1]
    before = jnp.sum(w * w, axis=-1, keepdims=True) / size + EPSILON
    after = jnp.sum(updated * updated, axis=-1, keepdims=True) / size + EPSILON
    out_ref[...] = (updated * (jnp.sqrt(before) / jnp.sqrt(after))).astype(BF16)


SIDE = 4
SHIFTS = ((1, 1), (3, 3), (1, 3), (3, 1), (2, 2), (2, 1), (1, 2), (3, 2),
          (2, 3), (0, 2), (2, 0), (0, 1), (1, 0), (0, 3), (3, 0), (0, 0))
GROUPS = (2, 6, 7, 1)
HEAD_AT, TARGET_AT = 0, 1
SOURCE_AT = TARGET_AT + len(SHIFTS)


def shifted(h, dx, dy):
    return (h // SIDE + dx) % SIDE * SIDE + (h + dy) % SIDE


def tail_kernel(k_ref, v_ref, tail_ref, table, sems):
    rows = pl.ds(k_ref.shape[0] - WINDOW, WINDOW)
    copies = [pltpu.make_async_copy(ref.at[rows], tail_ref.at[n], sems.at[n]) for n, ref in enumerate((k_ref, v_ref))]
    for c in copies:
        c.start()
    head = lax.axis_index("head")
    table[HEAD_AT] = head
    for n, (dx, dy) in enumerate(SHIFTS):
        table[TARGET_AT + n] = shifted(head, dx, dy)
        table[SOURCE_AT + n] = shifted(head, SIDE - dx, SIDE - dy)
    for c in copies:
        c.wait()


def tails(k, v):
    hd = k.shape[1]
    return pl.pallas_call(
        tail_kernel,
        in_specs=[pl.BlockSpec(memory_space=pl.ANY)] * 2,
        out_specs=[pl.BlockSpec(memory_space=pltpu.VMEM), pl.BlockSpec(memory_space=pltpu.SMEM)],
        out_shape=[pltpu.VMEM((2, WINDOW, hd), BF16), jax.ShapeDtypeStruct((SOURCE_AT + len(SHIFTS),), jnp.int32)],
        scratch_shapes=[pltpu.SemaphoreType.DMA((2,))],
        compiler_params=pltpu.CompilerParams(vmem_limit_bytes=60 << 20),
        name="tails",
    )(k, v)


def softmax_parts(s, lo, scale):
    tq, span = s.shape[0], s.shape[1]
    row = lax.broadcasted_iota(jnp.int32, (tq, tq), 0)
    col = lax.broadcasted_iota(jnp.int32, (tq, tq), 1)
    if lo is not None:
        s = jnp.where(lax.broadcasted_iota(jnp.int32, (tq, span), 1) >= lo, s, -1e30)
    parts = [jnp.where(col > row, s[:, :tq], -1e30), s[:, tq:WINDOW], jnp.where(col <= row, s[:, WINDOW:], -1e30)]
    top = jnp.maximum(jnp.max(jnp.maximum(parts[0], parts[2]), axis=1, keepdims=True),
                      jnp.max(parts[1], axis=1, keepdims=True)) * scale
    p = jnp.concatenate([jnp.exp2(x * scale - top) for x in parts], axis=1)
    return p.astype(BF16), 1.0 / jnp.sum(p, axis=1, keepdims=True)


def attend(q_rows, o_store, key_rows, value_rows, lo, count, scale):
    scores = dot_nt(q_rows(0), key_rows(0))
    for n in range(count):
        ahead = dot_nt(q_rows(n + 1), key_rows(n + 1)) if n + 1 < count else None
        p, inverse = softmax_parts(scores, None if lo is None else lo(n), scale)
        o_store(n, (dot_nn(p, value_rows(n)) * inverse).astype(BF16))
        scores = ahead


def attention_own_kernel(q_ref, k_ref, v_ref, *refs, tq, per, start, stop, scale):
    o_ref = refs[-1]

    def one(t, carry):
        first = start + t * per * tq

        def rows(ref, size, back):
            return lambda n: ref[pl.ds(pl.multiple_of(first + n * tq - back, tq), size), :]

        def store(n, x):
            o_ref[pl.ds(pl.multiple_of(first + n * tq, tq), tq), :] = x

        attend(rows(q_ref, tq, 0), store, rows(k_ref, WINDOW + tq, WINDOW), rows(v_ref, WINDOW + tq, WINDOW),
               None, per, scale)
        return carry

    lax.fori_loop(0, (stop - start) // (per * tq), one, 0)


def attention_first_kernel(q_ref, b_ref, k_ref, v_ref, _, o_ref, *, tq, scale):
    z, core = position()
    limit = jnp.where(z + core == 0, WINDOW, 0)

    def window(which, ref):
        return lambda n: jnp.concatenate([b_ref[which, n * tq:, :], ref[:(n + 1) * tq, :]], axis=0)

    def store(n, x):
        o_ref[n * tq:(n + 1) * tq, :] = x

    attend(lambda n: q_ref[n * tq:(n + 1) * tq, :], store, window(0, k_ref), window(1, v_ref),
           lambda n: limit - n * tq, WINDOW // tq, scale)


INSIDE = pl.BlockSpec(memory_space=pltpu.VMEM)


def attention_own(q, k, v, start, stop, attended=None, tq=256, per=2):
    rows, hd = q.shape
    into = [] if attended is None else [attended]
    return pl.pallas_call(
        functools.partial(attention_own_kernel, tq=tq, per=per, start=start, stop=stop, scale=hd ** -0.5 * LOG2E),
        in_specs=[INSIDE] * (3 + len(into)),
        out_specs=INSIDE,
        out_shape=pltpu.VMEM((rows, hd), BF16),
        input_output_aliases={3: 0} if into else {},
        cost_estimate=pl.CostEstimate(flops=4 * (stop - start) * (WINDOW + tq) * hd,
                                      bytes_accessed=8 << 20, transcendentals=(stop - start) * WINDOW),
        compiler_params=pltpu.CompilerParams(vmem_limit_bytes=14 << 20),
        name="attention_own",
    )(q, k, v, *into)


def attention_first(q, before, k, v, attended, tq=256):
    hd = q.shape[1]
    return pl.pallas_call(
        functools.partial(attention_first_kernel, tq=tq, scale=hd ** -0.5 * LOG2E),
        in_specs=[INSIDE] * 5,
        out_specs=INSIDE,
        out_shape=pltpu.VMEM(attended.shape, BF16),
        input_output_aliases={4: 0},
        cost_estimate=pl.CostEstimate(flops=4 * WINDOW * (WINDOW + tq) * hd,
                                      bytes_accessed=6 << 20, transcendentals=WINDOW * WINDOW),
        compiler_params=pltpu.CompilerParams(vmem_limit_bytes=18 << 20),
        name="attention_first",
    )(q, before, k, v, attended)


EXTRA = 8
LANES = 256


def apply_kernel(table, q_ref, attended_ref, gate_ref, gain_ref, *refs, count, n_pieces, at):
    weights, outs = refs[:n_pieces], refs[n_pieces:]
    if n_pieces > 1:
        wt, start = outs[-1], 0
        for p in weights:
            wt[:, start:start + p.shape[1], :] = p[...]
            start += p.shape[1]
    else:
        wt = weights[0]
    share, hd = q_ref.shape[1:]
    targets = [table[TARGET_AT + at + n] for n in range(count)]
    gain = gain_ref[:, pl.ds(pl.multiple_of(table[HEAD_AT] * hd, hd), hd)]
    q = jnp.concatenate([q_ref[t] for t in targets], axis=0)
    hidden = (silu(dot_nt(q, wt[0])) * dot_nt(q, wt[1])).astype(BF16)
    fast = dot_nn(hidden, wt[2])
    for n, t in enumerate(targets):
        rows = slice(n * share, (n + 1) * share)
        head = (attended_ref[t].astype(F32) + fast[rows]).astype(BF16).astype(F32)
        squares = jnp.sum(head * head, axis=1, keepdims=True)
        y = outs[n]
        y[:share, :] = (head * (gain * silu(gate_ref[t].astype(F32)))).astype(BF16)
        column = jnp.concatenate([squares, jnp.zeros((LANES - share, 1), F32)], axis=0)
        line = jnp.broadcast_to(column, (LANES, 128)).T[:EXTRA, :]
        high = line.astype(BF16)
        low = (line - high.astype(F32)).astype(BF16)
        y[share:, :LANES] = high
        y[share:, LANES:] = low


def applied(table, q, attended, out_gate, gain, weights, n_head, at, count):
    rows, hd = q.shape
    share = rows // n_head
    fh = sum(p.shape[1] for p in weights)
    blocks = [a.reshape(n_head, share, hd) for a in (q, attended, out_gate)]
    inside = pl.BlockSpec(memory_space=pltpu.VMEM)
    outs = [pltpu.VMEM((share + EXTRA, hd), BF16)] * count
    if len(weights) > 1:
        outs.append(pltpu.VMEM((3, fh, hd), BF16))
    return pl.pallas_call(
        functools.partial(apply_kernel, count=count, n_pieces=len(weights), at=at),
        in_specs=[pl.BlockSpec(memory_space=pltpu.SMEM)] + [inside] * (4 + len(weights)),
        out_specs=[inside] * len(outs),
        out_shape=outs,
        cost_estimate=pl.CostEstimate(flops=6 * count * share * hd * fh, bytes_accessed=count << 20,
                                      transcendentals=2 * count * share * fh),
        compiler_params=pltpu.CompilerParams(vmem_limit_bytes=18 << 20),
        name="apply_fast",
    )(table, *blocks, gain, *weights)


def scale_kernel(table, *refs):
    count = (len(refs) - 2) // 1 - 1
    y_refs, (o_ref, buf, sems) = refs[:count], refs[count:]
    share, width = buf.shape[1:]
    s = y_refs[0][share:, :].astype(F32)
    for y in y_refs[1:]:
        s = s + y[share:, :].astype(F32)
    line = s[:, :LANES] + s[:, LANES:]
    r = lax.rsqrt(line / (count * width) + EPSILON)
    r = jnp.concatenate([r] * (128 // EXTRA), axis=0).T[:share, :]
    r = jnp.concatenate([r] * (width // 128), axis=1)
    copies = []
    for n in range(count):
        buf[n] = (y_refs[n][:share, :].astype(F32) * r).astype(BF16)
        columns = pl.ds(pl.multiple_of(table[SOURCE_AT + n] * width, width), width)
        copies.append(pltpu.make_async_copy(buf.at[n], o_ref.at[:, columns], sems.at[n]))
        copies[-1].start()
    for c in copies:
        c.wait()


def scaled_rows(table, parts):
    rows, hd = parts[0].shape
    share, count = rows - EXTRA, len(parts)
    return pl.pallas_call(
        scale_kernel,
        in_specs=[pl.BlockSpec(memory_space=pltpu.SMEM)] + [pl.BlockSpec(memory_space=pltpu.VMEM)] * count,
        out_specs=pl.BlockSpec(memory_space=pl.ANY),
        out_shape=jax.ShapeDtypeStruct((share, count * hd), BF16),
        scratch_shapes=[pltpu.VMEM((count, share, hd), BF16), pltpu.SemaphoreType.DMA((count,))],
        compiler_params=pltpu.CompilerParams(vmem_limit_bytes=12 << 20),
        name="scale_rows",
    )(table, *parts)


def layer(queries, key_vectors, value_vectors, step_sizes, w_in, w_up, w_out, out_gate, norm_gain):
    rows, _ = queries.shape
    n_ctx, n_head = lax.axis_size("ctx"), lax.axis_size("head")
    z_size = n_ctx // 2
    tied = lax.optimization_barrier

    def along_z(x, d):
        return lax.ppermute(x, "ctx", [(i, ((i // 2 + d) % z_size) * 2 + i % 2) for i in range(n_ctx)])

    def swapped(x):
        return lax.ppermute(x, "ctx", [(i, i ^ 1) for i in range(n_ctx)])

    tail, table = tails(key_vectors, value_vectors)
    before = lax.ppermute(tail, "ctx", [(i, i + 1) for i in range(n_ctx - 1)])
    early = [pltpu.with_memory_space_constraint(x, pltpu.VMEM) for x in (step_sizes, w_in, w_up, w_out)]
    keep, send, w_slice, keys, values = increments(key_vectors, value_vectors, *early, z_size)

    order = sorted(range(1, z_size), key=lambda d: -min(d, z_size - d))
    parts = pair_sum(keep, swapped(send), z_size)
    below = z_size - 1
    from_far, from_below = along_z(parts[2], below), along_z(parts[1], 1)
    q, own = tied((queries, parts[0]))
    half = rows - WINDOW
    attended = attention_own(q, keys, values, WINDOW, half)
    attended, from_far = tied((attended, from_far))
    both = small_call(add_kernel, jax.ShapeDtypeStruct(own.shape, BF16), parts[below], from_far)
    from_above = along_z(both, below)
    q, own, _ = tied((queries, own, both))
    attended = attention_own(q, keys, values, half, rows, attended)
    attended, from_below, from_above = tied((attended, from_below, from_above))
    piece = small_call(renorm_kernel, jax.ShapeDtypeStruct(own.shape, BF16),
                       w_slice, own, from_below, from_above)
    rest = [along_z(piece, d) for d in order]
    q, piece = tied((queries, piece))
    attended = attention_first(q, before, keys, values, attended)
    attended, rest = tied((attended, rest))
    chip = [piece] + rest
    other = [swapped(p) for p in chip]

    weights, gain = chip + other, norm_gain.reshape(1, -1)
    parts, at = [], 0
    for count in GROUPS:
        outs = applied(table, queries, attended, out_gate, gain, weights, n_head, at, count)
        if len(outs) > count:
            weights = outs[count:]
        for y, (dx, dy) in zip(outs, SHIFTS[at:at + count]):
            if dx or dy:
                y = lax.ppermute(y, "head", [(h, shifted(h, dx, dy)) for h in range(n_head)])
            parts.append(y)
        at += count
    return scaled_rows(table, parts)


def solution(mesh):
    return jax.shard_map(
        layer,
        mesh=mesh,
        in_specs=(
            P("ctx", "head"), P("ctx", "head"), P("ctx", "head"), P("head", "ctx"),
            P("head", None, None), P("head", None, None), P("head", None, None),
            P("ctx", "head"), P(),
        ),
        out_specs=P(("ctx", "head"), None),
        check_vma=False,
    )
```
